128 devices in a mesh: rx: 8 (over x, core), ry: 16 (over y, z).
Axes of the slice: x: 4, y: 4, z: 4, core: 2. Of those that a mesh axis runs over, the one named last changes fastest.
Arguments:
- column_features: bfloat16 [16384, 1536], P(('rx', 'ry')), may hold values from -6 to 6
- column_route: int32 [16384], P(('rx', 'ry')), may hold values from 0 to 32767, as said below
- cotangent: bfloat16 [128, 256, 1536], P('rx', 'ry'), may hold values from -6 to 6
- first_weight: bfloat16 [27, 96, 96], replicated, may hold values from -0.125 to 0.125
- second_weight: bfloat16 [27, 96, 96], replicated, may hold values from -0.125 to 0.125
Outputs:
- block_output: bfloat16 [128, 256, 1536], P('rx', 'ry')
- feature_grads: bfloat16 [16384, 1536], P(('rx', 'ry'))
- first_grad: float32 [27, 96, 96], replicated
- second_grad: float32 [27, 96, 96], replicated
The draws below stay inside these ranges and needn't reach their ends.
Inputs may be any that keep to these rules, and one draw needn't show every extreme that they name: `column_route`: entries are distinct; entry o * 256 + q names slot q of owner o, owner o = i * 16 + j being the device at rx index i and ry index j. The columns of one owner are spread over the devices' shards as evenly as possible: each shard holds the floor or the ceiling of that owner's count / 128. An owner holds at most 256 columns, and in every draw one owner holds exactly 256, so that it receives 2 from every shard.
All inputs are finite; a program needn't handle non-finite values.
Results may differ from the reference program's by a relative error of at most 0.0029.
Values may be sent and summed in bfloat16 or wider, within the bound.
A program may use at most 256 MiB of HBM per device.

```python
import jax
import jax.numpy as jnp
from jax import lax

C = 96
RX = 16
RY = 16
RZ = 16
SLOTS = 256
TILES_DEV = 128
TILES = 16384
NXV = 128
NYV = 256
N_RX = 8
N_RY = 16
DEVICES = 128


def draw_column_route(key, part):
    devices_all = DEVICES
    per_shard = TILES_DEV
    region_slots = SLOTS
    overall = devices_all * per_shard
    keys = jax.random.split(jax.random.fold_in(key, 17), 5)
    halfway = devices_all // 2
    surplus = jax.random.randint(keys[0], (halfway,), 0, per_shard + 1).astype(jnp.int32)
    surplus = surplus.at[0].set(per_shard)
    loads = jnp.concatenate([per_shard + surplus, per_shard - surplus]).astype(jnp.int32)
    owner_order = jax.random.permutation(keys[1], devices_all).astype(jnp.int32)
    ends = jnp.cumsum(loads).astype(jnp.int32)
    position = jnp.arange(overall, dtype=jnp.int32)
    which = jnp.searchsorted(ends, position, side='right').astype(jnp.int32)
    starts = ends[which] - loads[which]
    within = position - starts
    owners = owner_order[which]
    slot_scores = jax.random.randint(keys[2], (devices_all, region_slots), 0, 1 << 14).astype(jnp.int32) * region_slots + jnp.arange(region_slots, dtype=jnp.int32)[None, :]
    slot_perm = jnp.argsort(slot_scores, axis=1).astype(jnp.int32)
    slot_of = slot_perm[owners, within]
    offset = jax.random.randint(keys[3], (), 0, devices_all).astype(jnp.int32)
    source = (position + offset) % devices_all
    ordinal = position // devices_all
    shard_scores = jax.random.randint(keys[4], (devices_all, per_shard), 0, 1 << 14).astype(jnp.int32) * per_shard + jnp.arange(per_shard, dtype=jnp.int32)[None, :]
    shard_perm = jnp.argsort(shard_scores, axis=1).astype(jnp.int32)
    index_in_shard = shard_perm[source, ordinal]
    target = owners * region_slots + slot_of
    result = jnp.zeros((overall,), jnp.int32).at[source * per_shard + index_in_shard].set(target)
    return result.astype(jnp.int32)


def levels(rng, extent, cuts, low, largest):
    gain, own = 1.0, jax.random.fold_in(rng, 6)
    for dim, blocks in cuts:
        steps = jnp.exp(jax.random.uniform(jax.random.fold_in(own, dim), (blocks,), jnp.float32, low / len(cuts), largest / len(cuts)))
        gain = gain * jnp.repeat(steps, extent[dim] // blocks).reshape([-1 if axis == dim else 1 for axis in range(len(extent))])
    return gain


def centred(stream_key, extent, scale, most, shards=(), held_as=jnp.bfloat16):
    array = jax.random.normal(stream_key, extent, jnp.float32) * scale
    if len(shards) > 0:
        array = levels(stream_key, extent, shards, -0.22, 0.18) * array
    return jnp.clip(array, min=-most, max=most).astype(held_as)


def setup_inputs(seed: int = 0) -> dict:
    arg_keys = jax.random.split(jax.random.key(seed), 6)
    return {
        "column_features": centred(arg_keys[0], (TILES, C * RZ), 1.0, 6.0, ((0, 128),)),
        "column_route": draw_column_route(jax.random.fold_in(arg_keys[5], 71), 0),
        "cotangent": centred(arg_keys[2], (NXV, NYV, C * RZ), 1.0, 6.0, ((0, 8), (1, 16))),
        "first_weight": centred(arg_keys[3], (27, C, C), (27 * C) ** -0.5, 0.125),
        "second_weight": centred(arg_keys[4], (27, C, C), (27 * C) ** -0.5, 0.125),
    }


def pad_field(field):
    return jnp.pad(field, ((1, 1), (1, 1), (0, 0), (1, 1)))

def conv_sum(padded, weights):
    size_x = padded.shape[0] - 2
    size_y = padded.shape[1] - 2
    size_z = padded.shape[3] - 2
    result = jnp.zeros((size_x, size_y, weights.shape[1], size_z), jnp.float32)
    for a in range(3):
        for b in range(3):
            for c in range(3):
                piece = padded[a:a + size_x, b:b + size_y, :, c:c + size_z].astype(jnp.float32)
                result = result + jnp.einsum('oi,xyiz->xyoz', weights[9 * a + 3 * b + c].astype(jnp.float32), piece, precision=lax.Precision.HIGHEST)
    return result

def correlate(grads, padded):
    size_x, size_y, _, size_z = grads.shape
    grads_f = grads.astype(jnp.float32)
    terms = []
    for a in range(3):
        for b in range(3):
            for c in range(3):
                piece = padded[a:a + size_x, b:b + size_y, :, c:c + size_z].astype(jnp.float32)
                terms.append(jnp.einsum('xyoz,xyiz->oi', grads_f, piece, precision=lax.Precision.HIGHEST))
    return jnp.stack(terms, axis=0)

def flipped(weights):
    return jnp.transpose(weights[::-1], (0, 2, 1))

def to_grid(rows, width):
    shaped = rows.reshape(N_RX, N_RY, RX, RY, width)
    return jnp.transpose(shaped, (0, 2, 1, 3, 4)).reshape(N_RX * RX, N_RY * RY, width)

def from_grid(field, width):
    shaped = field.reshape(N_RX, RX, N_RY, RY, width)
    return jnp.transpose(shaped, (0, 2, 1, 3, 4)).reshape(N_RX * N_RY * RX * RY, width)

def reference(column_features, column_route, cotangent, first_weight, second_weight):
    devices_all = N_RX * N_RY
    row_width = C * RZ
    columns = jnp.zeros((devices_all * SLOTS, row_width), jnp.bfloat16).at[column_route].set(column_features)
    active = jnp.zeros((devices_all * SLOTS, 1), jnp.float32).at[column_route].set(1.0)
    field = to_grid(columns, row_width).reshape(NXV, NYV, C, RZ)
    mask = to_grid(active, 1).reshape(NXV, NYV, 1, 1)
    padded_x = pad_field(field)
    hidden = mask * conv_sum(padded_x, first_weight)
    act = jax.nn.silu(hidden).astype(jnp.bfloat16)
    padded_a = pad_field(act)
    second = conv_sum(padded_a, second_weight)
    block_output = (field.astype(jnp.float32) + mask * second).astype(jnp.bfloat16).reshape(NXV, NYV, row_width)
    cot_field = cotangent.reshape(NXV, NYV, C, RZ).astype(jnp.float32)
    outer_grad = (mask * cot_field).astype(jnp.bfloat16)
    act_grad = conv_sum(pad_field(outer_grad), flipped(second_weight))
    sigma = jax.nn.sigmoid(hidden)
    hidden_grad = (mask * act_grad * sigma * (1.0 + hidden * (1.0 - sigma))).astype(jnp.bfloat16)
    grid_grad = (mask * cot_field + conv_sum(pad_field(hidden_grad), flipped(first_weight))).astype(jnp.bfloat16)
    back_rows = from_grid(grid_grad.reshape(NXV, NYV, row_width), row_width)
    feature_grads = back_rows[column_route]
    factor = 1.0 / jnp.sqrt(jnp.float32(devices_all * TILES_DEV * RZ))
    second_grad = correlate(outer_grad, padded_a) * factor
    first_grad = correlate(hidden_grad, padded_x) * factor
    return (block_output, feature_grads, first_grad, second_grad)
```

```python
import functools

import jax
import jax.numpy as jnp
from jax import lax
from jax.experimental import pallas as pl
from jax.experimental.pallas import tpu as pltpu
from jax.sharding import PartitionSpec as P

F32 = jnp.float32
BF16 = jnp.bfloat16
LANES = 128
VMEM_LIMIT = 64 * 1000 * 1000


def params():
    return pltpu.CompilerParams(vmem_limit_bytes=VMEM_LIMIT)


def iota(shape, dim):
    return lax.broadcasted_iota(jnp.int32, shape, dim)


def spread_columns(rows, scratch, put, depth):
    width = rows.shape[1]
    count = rows.shape[0]
    for zp in range(depth // 2):
        k = iota((width, 2 * LANES), 0)
        n = iota((width, 2 * LANES), 1)
        want = (n % LANES) * depth + 2 * zp + n // LANES
        table = jnp.where(k == want, 1.0, 0.0).astype(BF16)
        moved = jnp.dot(rows, table, preferred_element_type=F32)
        scratch[pl.ds(2 * zp, count, stride=depth), :] = moved[:, :LANES]
        scratch[pl.ds(2 * zp + 1, count, stride=depth), :] = moved[:, LANES:]


def gather_columns(scratch, count, depth, width):
    total = jnp.zeros((count, width), F32)
    for zp in range(depth // 2):
        n = iota((2 * LANES, width), 0)
        k = iota((2 * LANES, width), 1)
        want = (n % LANES) * depth + 2 * zp + n // LANES
        table = jnp.where(k == want, 1.0, 0.0).astype(BF16)
        pair = jnp.concatenate(
            [
                scratch[pl.ds(2 * zp, count, stride=depth), :],
                scratch[pl.ds(2 * zp + 1, count, stride=depth), :],
            ],
            axis=1,
        ).astype(BF16)
        total = total + jnp.dot(pair, table, preferred_element_type=F32)
    return total.astype(BF16)


def shift_planes(src, dst):
    count_x, count_y, depth, lanes = src.shape
    z = iota((count_y * depth, lanes), 0) % depth

    def body(x, carry):
        plane = src[x]
        v = plane.astype(F32).reshape(count_y * depth, lanes)
        below = pltpu.roll(v, 1, 0)
        above = pltpu.roll(v, count_y * depth - 1, 0)
        dst[0, x] = jnp.where(z == 0, 0.0, below).astype(BF16).reshape(count_y, depth, lanes)
        dst[1, x] = plane
        dst[2, x] = jnp.where(z == depth - 1, 0.0, above).astype(BF16).reshape(
            count_y, depth, lanes
        )
        return carry

    lax.fori_loop(0, count_x, body, 0)


def pair_weights(weights, table, transposed):
    table[...] = jnp.zeros(table.shape, BF16)
    channels = weights.shape[1]
    for a in range(3):
        for b in range(3):
            for c in range(3):
                tap = 9 * a + 3 * b + c
                if transposed:
                    block = weights[tap].astype(F32).T.astype(BF16)
                else:
                    block = weights[26 - tap]
                for p in range(2):
                    row = ((a + p) * 9 + 3 * b + c) * LANES
                    table[row : row + channels, p * LANES : p * LANES + channels] = block


def pair_patches(planes, xp, count_y):
    depth = planes.shape[3]
    pieces = []
    for j in range(4):
        for b in range(3):
            for c in range(3):
                pieces.append(
                    planes[c, 2 * xp + j, b : b + count_y].reshape(count_y * depth, LANES)
                )
    return jnp.concatenate(pieces, axis=1)


def pair_conv(planes, table, xp, count_y):
    return jnp.dot(
        pair_patches(planes, xp, count_y), table[...], preferred_element_type=F32
    )


def correlate(local, planes, turned, out, flip):
    count_x, count_y, depth, _ = local.shape
    rows = count_y * depth
    for xp in range(count_x // 2):
        pair = jnp.concatenate(
            [
                local[2 * xp].reshape(rows, LANES),
                local[2 * xp + 1].reshape(rows, LANES),
            ],
            axis=1,
        )
        turned[:, xp * rows : (xp + 1) * rows] = pair.astype(F32).T.astype(BF16)
    out[...] = jnp.zeros(out.shape, F32)

    def body(step, carry):
        jj = (step // 3) * 2
        b = step % 3
        pieces = []
        for dj in range(2):
            for c in range(3):
                pieces.append(
                    jnp.concatenate(
                        [
                            planes[c, 2 * xp + jj + dj, pl.ds(b, count_y)].reshape(rows, LANES)
                            for xp in range(count_x // 2)
                        ],
                        axis=0,
                    )
                )
        for half in range(3):
            both = jnp.concatenate([pieces[2 * half], pieces[2 * half + 1]], axis=1)
            prod = jnp.dot(turned[...], both, preferred_element_type=F32)
            for s in range(2):
                dj, c = divmod(2 * half + s, 3)
                for p in range(2):
                    a = jj + dj - p
                    val = prod[p * LANES : (p + 1) * LANES, s * LANES : (s + 1) * LANES]
                    slot = (a + 1) * 9 + 3 * b + c
                    out[slot] += val
        return carry

    lax.fori_loop(0, 6, body, 0)


def enter_kernel(in_ref, slots_ref, cot_ref, x_ref, g_ref, mask_ref, scratch):
    depth = x_ref.shape[2]
    slots, width = cot_ref.shape
    count = in_ref.shape[0]
    hot = (slots_ref[...] == iota((slots, count), 0)).astype(F32)
    active = jnp.sum(hot, axis=1, keepdims=True)
    rows = jnp.dot(
        hot.astype(BF16), in_ref[:, :width], preferred_element_type=F32
    ).astype(BF16)
    spread_columns(rows, scratch, None, depth)
    x_ref[...] = scratch[...].astype(BF16).reshape(x_ref.shape)
    masked = (cot_ref[...].astype(F32) * active).astype(BF16)
    spread_columns(masked, scratch, None, depth)
    g_ref[...] = scratch[...].astype(BF16).reshape(g_ref.shape)
    wide = jnp.broadcast_to(active, (slots, LANES))
    for z in range(depth):
        scratch[pl.ds(z, slots, stride=depth), :] = wide
    mask_ref[...] = scratch[...].astype(BF16).reshape(mask_ref.shape)


def middle_kernel(
    xh_ref, gh_ref, mask_ref, w1_ref, w2_ref,
    act_ref, hg_ref, dw1_ref, dw2_ref,
    x3, g3, t1, t2, turned,
):
    count_x, count_y, depth, _ = act_ref.shape
    rows = count_y * depth
    shift_planes(xh_ref, x3)
    shift_planes(gh_ref, g3)
    pair_weights(w1_ref, t1, True)
    pair_weights(w2_ref, t2, False)

    def body(xp, carry):
        hidden2 = pair_conv(x3, t1, xp, count_y)
        grad2 = pair_conv(g3, t2, xp, count_y)
        for p in range(2):
            x = 2 * xp + p
            mask = mask_ref[x].reshape(rows, LANES).astype(F32)
            hidden = mask * hidden2[:, p * LANES : (p + 1) * LANES]
            grad = grad2[:, p * LANES : (p + 1) * LANES]
            s = 1.0 / (1.0 + jnp.exp(-hidden))
            act_ref[x] = (hidden * s).astype(BF16).reshape(count_y, depth, LANES)
            hg = mask * grad * s * (1.0 + hidden * (1.0 - s))
            hg_ref[x] = hg.astype(BF16).reshape(count_y, depth, LANES)
        return carry

    lax.fori_loop(0, count_x // 2, body, 0)
    correlate(hg_ref, x3, turned, dw1_ref, False)
    correlate(act_ref, g3, turned, dw2_ref, True)


def leave_kernel(
    ah_ref, hh_ref, x_ref, g_ref, mask_ref, slots_ref, w1_ref, w2_ref,
    out_ref, back_ref,
    a3, h3, t1, t2, s_out, s_grad,
):
    count_x, count_y, depth, _ = x_ref.shape
    rows = count_y * depth
    slots, width = out_ref.shape
    shift_planes(ah_ref, a3)
    shift_planes(hh_ref, h3)
    pair_weights(w2_ref, t2, True)
    pair_weights(w1_ref, t1, False)

    def body(xp, carry):
        second2 = pair_conv(a3, t2, xp, count_y)
        grad2 = pair_conv(h3, t1, xp, count_y)
        for p in range(2):
            x = 2 * xp + p
            at = pl.ds(pl.multiple_of(x * rows, rows), rows)
            mask = mask_ref[x].reshape(rows, LANES).astype(F32)
            own = x_ref[x].reshape(rows, LANES).astype(F32)
            cot = g_ref[x].reshape(rows, LANES).astype(F32)
            s_out[at, :] = own + mask * second2[:, p * LANES : (p + 1) * LANES]
            s_grad[at, :] = cot + grad2[:, p * LANES : (p + 1) * LANES]
        return carry

    lax.fori_loop(0, count_x // 2, body, 0)
    out_ref[...] = gather_columns(s_out, slots, depth, width)
    grads = gather_columns(s_grad, slots, depth, width)
    count = slots_ref.shape[0]
    hot = (slots_ref[...] == iota((count, slots), 1)).astype(F32).astype(BF16)
    back_ref[...] = jnp.dot(hot, grads, preferred_element_type=F32).astype(BF16)


def extended(block, sides, width):
    for axis, dim in sides:
        count = lax.axis_size(axis)
        forward = [(i, i + 1) for i in range(count - 1)]
        backward = [(target, source) for source, target in forward]
        low = lax.ppermute(
            lax.slice_in_dim(block, block.shape[dim] - width, None, axis=dim), axis, forward
        )
        high = lax.ppermute(lax.slice_in_dim(block, 0, width, axis=dim), axis, backward)
        block = jnp.concatenate([low, block, high], axis=dim)
    return block


def on_device(column_features, column_route, cotangent, first_weight, second_weight):
    count_x = lax.axis_size("rx")
    count_y = lax.axis_size("ry")
    count_all = count_x * count_y
    shard_rows, row_width = column_features.shape
    region_x, region_y = cotangent.shape[:2]
    channels = first_weight.shape[1]
    depth = row_width // channels
    region_slots = region_x * region_y
    capacity = 2 * shard_rows // count_all
    capacity_all = count_all * capacity
    owners = column_route // region_slots
    slot_ids = column_route % region_slots
    shard_index = jnp.arange(shard_rows, dtype=jnp.int32)
    earlier = shard_index[:, None] > shard_index[None, :]
    same_owner = owners[:, None] == owners[None, :]
    ranks = jnp.sum(jnp.logical_and(earlier, same_owner).astype(jnp.int32), axis=1)
    send_pos = owners * capacity + ranks
    buffer_index = jnp.arange(capacity_all, dtype=jnp.int32)
    send_hot = send_pos[:, None] == buffer_index[None, :]
    send_table = send_hot.astype(BF16)
    outgoing = jnp.einsum(
        "sr,sw->rw", send_table, column_features, preferred_element_type=F32
    ).astype(BF16)
    filled = jnp.sum(send_hot.astype(jnp.int32), axis=0)
    slot_total = jnp.sum(jnp.where(send_hot, slot_ids[:, None], 0), axis=0)
    out_slots = jnp.where(filled > 0, slot_total, region_slots).astype(BF16)
    outgoing = jnp.concatenate(
        [outgoing, jnp.broadcast_to(out_slots[:, None], (capacity_all, LANES))], axis=1
    )
    incoming = lax.all_to_all(
        outgoing.reshape(count_all, capacity, row_width + LANES),
        ("rx", "ry"),
        split_axis=0,
        concat_axis=0,
        tiled=True,
    ).reshape(capacity_all, row_width + LANES)
    in_slots = incoming[:, row_width].astype(jnp.int32)

    cot_rows = cotangent.reshape(region_slots, row_width)
    field = jax.ShapeDtypeStruct((region_x, region_y, depth, LANES), BF16)
    planes = pltpu.VMEM((3, region_x + 2, region_y + 2, depth, LANES), BF16)
    table = pltpu.VMEM((36 * LANES, 2 * LANES), BF16)
    voxels = region_slots * depth
    grad_shape = jax.ShapeDtypeStruct((45, LANES, LANES), F32)
    x_own, g_own, mask = pl.pallas_call(
        enter_kernel,
        out_shape=(field, field, field),
        scratch_shapes=[pltpu.VMEM((voxels, LANES), F32)],
        compiler_params=params(),
    )(incoming, in_slots[None, :], cot_rows)
    sides = (("rx", 0), ("ry", 1))
    xh = extended(x_own, sides, 1)
    gh = extended(g_own, sides, 1)
    act, hg, dw1, dw2 = pl.pallas_call(
        middle_kernel,
        out_shape=(field, field, grad_shape, grad_shape),
        scratch_shapes=[planes, planes, table, table, pltpu.VMEM((2 * LANES, voxels // 2), BF16)],
        compiler_params=params(),
    )(xh, gh, mask, first_weight, second_weight)
    ah = extended(act, sides, 1)
    hh = extended(hg, sides, 1)
    out_rows, back_rows = pl.pallas_call(
        leave_kernel,
        out_shape=(
            jax.ShapeDtypeStruct((region_slots, row_width), BF16),
            jax.ShapeDtypeStruct((capacity_all, row_width), BF16),
        ),
        scratch_shapes=[
            planes, planes, table, table,
            pltpu.VMEM((voxels, LANES), F32), pltpu.VMEM((voxels, LANES), F32),
        ],
        compiler_params=params(),
    )(ah, hh, x_own, g_own, mask, in_slots[:, None], first_weight, second_weight)
    returned = lax.all_to_all(
        back_rows.reshape(count_all, capacity, row_width),
        ("rx", "ry"),
        split_axis=0,
        concat_axis=0,
        tiled=True,
    ).reshape(capacity_all, row_width)
    feature_grads = jnp.dot(send_table, returned, preferred_element_type=F32).astype(BF16)

    first_local = dw1[9:36, :channels, :channels]
    second_local = jnp.transpose(dw2[9:36, :channels, :channels][::-1], (0, 2, 1))
    both = jnp.stack([first_local, second_local]).astype(BF16).reshape(count_all, -1)
    spread = lax.all_to_all(both, ("rx", "ry"), split_axis=0, concat_axis=0, tiled=True)
    share = jnp.sum(spread.astype(F32), axis=0).astype(BF16)
    whole = lax.all_gather(share, ("rx", "ry"), axis=0, tiled=True)
    factor = 1.0 / jnp.sqrt(F32(count_all * shard_rows * depth))
    scaled = (whole.astype(F32) * factor).reshape(2, 27, channels, channels)
    return (
        out_rows.reshape(region_x, region_y, row_width),
        feature_grads,
        scaled[0],
        scaled[1],
    )


def solution(mesh):
    in_specs = (P(("rx", "ry"), None), P(("rx", "ry")), P("rx", "ry", None), P(), P())
    out_specs = (P("rx", "ry", None), P(("rx", "ry"), None), P(), P())
    return jax.shard_map(
        on_device, mesh=mesh, in_specs=in_specs, out_specs=out_specs, check_vma=False
    )
```

```python
import functools

import jax
import jax.numpy as jnp
from jax import lax
from jax.experimental import pallas as pl
from jax.experimental.pallas import tpu as pltpu
from jax.sharding import PartitionSpec as P

F32 = jnp.float32
BF16 = jnp.bfloat16
LANES = 128
VMEM_LIMIT = 64 * 1024 * 1024 - 64 * 1024
SIDES = [(dx, dy) for dx in (-1, 0, 1) for dy in (-1, 0, 1) if (dx, dy) != (0, 0)]


def params():
    return pltpu.CompilerParams(vmem_limit_bytes=VMEM_LIMIT)


def iota(shape, dim):
    return lax.broadcasted_iota(jnp.int32, shape, dim)


def build_move(move, depth):
    width = move.shape[0]
    k = iota((width, 2 * LANES), 0)
    n = iota((width, 2 * LANES), 1)
    base = k - (n % LANES) * depth - n // LANES
    for zp in range(depth // 2):
        move[:, zp * 2 * LANES : (zp + 1) * 2 * LANES] = jnp.where(
            base == 2 * zp, 1.0, 0.0
        ).astype(BF16)


def spread_columns(rows, scale, move, scratch, depth):
    count = rows.shape[0]
    for zp in range(depth // 2):
        moved = jnp.dot(
            rows, move[:, zp * 2 * LANES : (zp + 1) * 2 * LANES], preferred_element_type=F32
        )
        if scale is not None:
            moved = moved * scale
        scratch[pl.ds(2 * zp, count, stride=depth), :] = moved[:, :LANES]
        scratch[pl.ds(2 * zp + 1, count, stride=depth), :] = moved[:, LANES:]


def gather_columns(scratch, move, count, depth):
    wide = jnp.concatenate(
        [scratch[pl.ds(z, count, stride=depth), :] for z in range(depth)], axis=1
    ).astype(BF16)
    return lax.dot_general(
        wide, move[...], (((1,), (1,)), ((), ())), preferred_element_type=F32
    ).astype(BF16)


def shift_block(planes, xs, ys):
    block = planes[1, xs, ys]
    count_x, count_y, depth, lanes = block.shape
    total = count_x * count_y * depth
    z = iota((total, lanes), 0) % depth
    v = block.astype(F32).reshape(total, lanes)
    below = jnp.where(z == 0, 0.0, pltpu.roll(v, 1, 0))
    above = jnp.where(z == depth - 1, 0.0, pltpu.roll(v, total - 1, 0))
    planes[0, xs, ys] = below.astype(BF16).reshape(block.shape)
    planes[2, xs, ys] = above.astype(BF16).reshape(block.shape)


def shift_inside(planes):
    rows, columns = planes.shape[1] - 2, planes.shape[2] - 2

    def body(x, carry):
        shift_block(planes, pl.ds(x + 1, 1), pl.ds(1, columns))
        return carry

    lax.fori_loop(0, rows, body, 0)


def shift_border(planes):
    rows, columns = planes.shape[1] - 2, planes.shape[2] - 2
    shift_block(planes, pl.ds(0, 1), pl.ds(0, columns + 2))
    shift_block(planes, pl.ds(rows + 1, 1), pl.ds(0, columns + 2))
    shift_block(planes, pl.ds(1, rows), pl.ds(0, 1))
    shift_block(planes, pl.ds(1, rows), pl.ds(columns + 1, 1))


def clear_border(planes):
    _, count_x, count_y, depth, lanes = planes.shape
    planes[1, 0] = jnp.zeros((count_y, depth, lanes), BF16)
    planes[1, count_x - 1] = jnp.zeros((count_y, depth, lanes), BF16)
    planes[1, :, 0] = jnp.zeros((count_x, depth, lanes), BF16)
    planes[1, :, count_y - 1] = jnp.zeros((count_x, depth, lanes), BF16)


def pair_weights(weights, table, transposed):
    channels = weights.shape[1]
    table[...] = jnp.zeros(table.shape, BF16)
    for a in range(3):
        for b in range(3):
            for c in range(3):
                tap = 9 * a + 3 * b + c
                if transposed:
                    block = weights[tap].astype(F32).T.astype(BF16)
                else:
                    block = weights[26 - tap]
                for p in range(2):
                    row = ((a + p) * 9 + 3 * b + c) * LANES
                    table[row : row + channels, p * LANES : p * LANES + channels] = block


def pair_conv(planes, table, xp, count_y):
    depth = planes.shape[3]
    pieces = []
    for j in range(4):
        for b in range(3):
            for c in range(3):
                pieces.append(
                    planes[c, 2 * xp + j, b : b + count_y].reshape(count_y * depth, LANES)
                )
    return jnp.dot(jnp.concatenate(pieces, axis=1), table[...], preferred_element_type=F32)


def correlate(local, planes, turned, out):
    _, count_x, count_y, depth, _ = local.shape
    count_x, count_y = count_x - 2, count_y - 2
    rows = count_y * depth
    for xp in range(count_x // 2):
        pair = jnp.concatenate(
            [
                local[1, 2 * xp + 1, 1 : count_y + 1].reshape(rows, LANES),
                local[1, 2 * xp + 2, 1 : count_y + 1].reshape(rows, LANES),
            ],
            axis=1,
        )
        turned[:, xp * rows : (xp + 1) * rows] = pair.astype(F32).T.astype(BF16)
    out[...] = jnp.zeros(out.shape, F32)

    def body(step, carry):
        jj = (step // 3) * 2
        b = step % 3
        pieces = []
        for dj in range(2):
            for c in range(3):
                pieces.append(
                    jnp.concatenate(
                        [
                            planes[c, 2 * xp + jj + dj, pl.ds(b, count_y)].reshape(rows, LANES)
                            for xp in range(count_x // 2)
                        ],
                        axis=0,
                    )
                )
        for half in range(3):
            both = jnp.concatenate([pieces[2 * half], pieces[2 * half + 1]], axis=1)
            prod = jnp.dot(turned[...], both, preferred_element_type=F32)
            for s in range(2):
                dj, c = divmod(2 * half + s, 3)
                for p in range(2):
                    slot = (jj + dj - p + 1) * 9 + 3 * b + c
                    out[slot] += prod[p * LANES : (p + 1) * LANES, s * LANES : (s + 1) * LANES]
        return carry

    lax.fori_loop(0, 6, body, 0)


def pack_grads(out, packed, base, flip, channels):
    tall = channels * channels // LANES
    rest = channels - tall
    lane = iota((tall, LANES), 1)

    def body(k, carry):
        block = out[9 + 26 - k].T if flip else out[9 + k]
        low = block[tall:channels]
        part = LANES - channels
        moved = jnp.concatenate(
            [pltpu.roll(low, channels - part * m, 1) for m in range(tall // rest)], axis=0
        )
        at = pl.ds(pl.multiple_of((base + k) * tall, 8), tall)
        packed[at, :] = jnp.where(lane < channels, block[:tall], moved)
        return carry

    lax.fori_loop(0, 27, body, 0)


def unpack_grads(packed, dest, base, factor, channels):
    tall = channels * channels // LANES
    rest = channels - tall
    part = LANES - channels
    lane = iota((rest, LANES), 1)

    def body(k, carry):
        v = packed[pl.ds(pl.multiple_of((base + k) * tall, 8), tall), :] * factor
        low = jnp.zeros((rest, LANES), F32)
        for m in range(tall // rest):
            turned = pltpu.roll(v[m * rest : (m + 1) * rest], (part * m - channels) % LANES, 1)
            low = jnp.where(lane // part == m, turned, low)
        dest[k, :tall, :] = v[:, :channels]
        dest[k, tall:, :] = low[:, :channels]
        return carry

    lax.fori_loop(0, 27, body, 0)


class Halo:
    def __init__(self, planes, send_sem, recv_sem, grid):
        self.planes, self.send_sem, self.recv_sem, self.grid = planes, send_sem, recv_sem, grid
        self.extent = (planes.shape[1] - 2, planes.shape[2] - 2)

    def copy(self, k):
        source, target = [], []
        for step, extent in zip(SIDES[k], self.extent):
            source.append({0: pl.ds(1, extent), 1: pl.ds(extent, 1), -1: pl.ds(1, 1)}[step])
            target.append({0: pl.ds(1, extent), 1: pl.ds(0, 1), -1: pl.ds(extent + 1, 1)}[step])
        (ix, iy, _, _), (dx, dy) = self.grid, SIDES[k]
        return pltpu.make_async_remote_copy(
            src_ref=self.planes.at[1, source[0], source[1]],
            dst_ref=self.planes.at[1, target[0], target[1]],
            send_sem=self.send_sem.at[k],
            recv_sem=self.recv_sem.at[k],
            device_id=(ix + dx, iy + dy),
            device_id_type=pl.DeviceIdType.MESH,
        )

    def there(self, dx, dy):
        ix, iy, nx, ny = self.grid
        return jnp.logical_and(
            jnp.logical_and(ix + dx >= 0, ix + dx < nx), jnp.logical_and(iy + dy >= 0, iy + dy < ny)
        )

    def start(self):
        for k, (dx, dy) in enumerate(SIDES):

            @pl.when(self.there(dx, dy))
            def _():
                self.copy(k).start()

    def wait(self):
        for k, (dx, dy) in enumerate(SIDES):

            @pl.when(self.there(-dx, -dy))
            def _():
                self.copy(k).wait_recv()

            @pl.when(self.there(dx, dy))
            def _():
                self.copy(k).wait_send()


def core_kernel(
    nx, ny, factor,
    in_ref, slot_row_ref, slot_col_ref, cot_ref, w1_ref, w2_ref,
    out_ref, back_ref, dw1_ref, dw2_ref,
    x3, g3, a3, h3, tx, tg, ta, th, move, s1, s2, mask_p, turned, grads,
    packed, shares, spread, whole,
    halo_send, halo_recv, sum_send, sum_recv,
):
    ix, iy = lax.axis_index("rx"), lax.axis_index("ry")
    count = nx * ny
    me = ix * ny + iy
    barrier = pltpu.get_barrier_semaphore()

    def peer(d):
        other = lax.rem(me + d, count)
        return (lax.div(other, ny), lax.rem(other, ny))

    for planes in (x3, g3, a3, h3):
        clear_border(planes)

    def greet(d, carry):
        pl.semaphore_signal(
            barrier, inc=1, device_id=peer(d), device_id_type=pl.DeviceIdType.MESH
        )
        return carry

    lax.fori_loop(1, count, greet, 0)
    _, count_x, count_y, depth, _ = x3.shape
    count_x, count_y = count_x - 2, count_y - 2
    rows = count_y * depth
    slots, width = cot_ref.shape
    channels = w1_ref.shape[1]
    grid = (ix, iy, nx, ny)
    halos = [
        Halo(planes, halo_send.at[k], halo_recv.at[k], grid)
        for k, planes in enumerate((x3, g3, a3, h3))
    ]
    inside = (pl.ds(1, count_x), pl.ds(1, count_y))
    build_move(move, depth)
    pair_weights(w1_ref, tx, True)
    pair_weights(w2_ref, tg, False)
    pair_weights(w2_ref, ta, True)
    pair_weights(w1_ref, th, False)

    hot = (slot_row_ref[...] == iota((slots, in_ref.shape[0]), 0)).astype(F32)
    active = jnp.sum(hot, axis=1, keepdims=True)
    spread_columns(cot_ref[...], active, move, s2, depth)
    g3[1, inside[0], inside[1]] = s2[...].astype(BF16).reshape(count_x, count_y, depth, LANES)
    pl.semaphore_wait(barrier, count - 1)
    halos[1].start()
    got = jnp.dot(hot.astype(BF16), in_ref[:, :width], preferred_element_type=F32).astype(BF16)
    spread_columns(got, None, move, s1, depth)
    x3[1, inside[0], inside[1]] = s1[...].astype(BF16).reshape(count_x, count_y, depth, LANES)
    halos[0].start()
    wide = jnp.broadcast_to(active, (slots, LANES))
    for z in range(depth):
        mask_p[pl.ds(z, slots, stride=depth), :] = wide
    shift_inside(g3)
    shift_inside(x3)
    halos[1].wait()
    shift_border(g3)
    halos[0].wait()
    shift_border(x3)

    def forward(xp, carry):
        hidden2 = pair_conv(x3, tx, xp, count_y)
        grad2 = pair_conv(g3, tg, xp, count_y)
        for p in range(2):
            x = 2 * xp + p
            mask = mask_p[pl.ds(pl.multiple_of(x * rows, rows), rows), :]
            hidden = mask * hidden2[:, p * LANES : (p + 1) * LANES]
            grad = grad2[:, p * LANES : (p + 1) * LANES]
            s = 1.0 / (1.0 + jnp.exp(-hidden))
            a3[1, x + 1, 1 : count_y + 1] = (
                (hidden * s).astype(BF16).reshape(count_y, depth, LANES)
            )
            hg = mask * grad * s * (1.0 + hidden * (1.0 - s))
            h3[1, x + 1, 1 : count_y + 1] = hg.astype(BF16).reshape(count_y, depth, LANES)
        return carry

    lax.fori_loop(0, count_x // 2, forward, 0)
    halos[2].start()
    halos[3].start()
    correlate(h3, x3, turned, grads)
    pack_grads(grads, packed, 0, False, channels)
    correlate(a3, g3, turned, grads)
    pack_grads(grads, packed, 27, True, channels)
    used = 54 * channels * channels // LANES
    packed[used:, :] = jnp.zeros((packed.shape[0] - used, LANES), F32)
    shares[...] = packed[...].astype(BF16).reshape(shares.shape)

    def send_share(d, carry):
        other = lax.rem(me + d, count)
        pltpu.make_async_remote_copy(
            src_ref=shares.at[other],
            dst_ref=spread.at[d - 1],
            send_sem=sum_send.at[0],
            recv_sem=sum_recv.at[0],
            device_id=peer(d),
            device_id_type=pl.DeviceIdType.MESH,
        ).start()
        return carry

    lax.fori_loop(1, count, send_share, 0)
    shift_inside(a3)
    shift_inside(h3)
    halos[2].wait()
    halos[3].wait()
    shift_border(a3)
    shift_border(h3)

    def backward(xp, carry):
        second2 = pair_conv(a3, ta, xp, count_y)
        grad2 = pair_conv(h3, th, xp, count_y)
        for p in range(2):
            x = 2 * xp + p
            at = pl.ds(pl.multiple_of(x * rows, rows), rows)
            own = x3[1, x + 1, 1 : count_y + 1].reshape(rows, LANES).astype(F32)
            cot = g3[1, x + 1, 1 : count_y + 1].reshape(rows, LANES).astype(F32)
            s1[at, :] = own + mask_p[at, :] * second2[:, p * LANES : (p + 1) * LANES]
            s2[at, :] = cot + grad2[:, p * LANES : (p + 1) * LANES]
        return carry

    lax.fori_loop(0, count_x // 2, backward, 0)

    pltpu.make_async_copy(spread, spread, sum_recv.at[0]).wait()
    pltpu.make_async_copy(spread, spread, sum_send.at[0]).wait()
    own_share = shares[me].astype(F32)
    total = lax.fori_loop(
        0, count - 1, lambda d, acc: acc + spread[d].astype(F32), own_share
    )
    whole[me] = total.astype(BF16)

    def send_total(d, carry):
        pltpu.make_async_remote_copy(
            src_ref=whole.at[me],
            dst_ref=whole.at[me],
            send_sem=sum_send.at[1],
            recv_sem=sum_recv.at[1],
            device_id=peer(d),
            device_id_type=pl.DeviceIdType.MESH,
        ).start()
        return carry

    lax.fori_loop(1, count, send_total, 0)

    grad_rows = gather_columns(s2, move, slots, depth)
    back_hot = (slot_col_ref[...] == iota((in_ref.shape[0], slots), 1)).astype(F32).astype(BF16)
    back_ref[...] = jnp.dot(back_hot, grad_rows, preferred_element_type=F32).astype(BF16)
    out_ref[...] = gather_columns(s1, move, slots, depth)

    pltpu.make_async_copy(spread, spread, sum_recv.at[1]).wait()
    pltpu.make_async_copy(spread, spread, sum_send.at[1]).wait()
    packed[...] = whole[...].astype(F32).reshape(packed.shape)
    unpack_grads(packed, dw1_ref, 0, factor, channels)
    unpack_grads(packed, dw2_ref, 27, factor, channels)


def on_device(column_features, column_route, cotangent, first_weight, second_weight):
    count_x = lax.axis_size("rx")
    count_y = lax.axis_size("ry")
    count_all = count_x * count_y
    shard_rows, row_width = column_features.shape
    region_x, region_y = cotangent.shape[:2]
    channels = first_weight.shape[1]
    depth = row_width // channels
    region_slots = region_x * region_y
    capacity = 2 * shard_rows // count_all
    capacity_all = count_all * capacity
    owners = column_route // region_slots
    slot_ids = column_route % region_slots
    shard_index = jnp.arange(shard_rows, dtype=jnp.int32)
    earlier = shard_index[:, None] > shard_index[None, :]
    same_owner = owners[:, None] == owners[None, :]
    ranks = jnp.sum(jnp.logical_and(earlier, same_owner).astype(jnp.int32), axis=1)
    send_pos = owners * capacity + ranks
    buffer_index = jnp.arange(capacity_all, dtype=jnp.int32)
    send_hot = send_pos[:, None] == buffer_index[None, :]
    send_table = send_hot.astype(BF16)
    outgoing = jnp.einsum(
        "sr,sw->rw", send_table, column_features, preferred_element_type=F32
    ).astype(BF16)
    filled = jnp.sum(send_hot.astype(jnp.int32), axis=0)
    slot_total = jnp.sum(jnp.where(send_hot, slot_ids[:, None], 0), axis=0)
    out_slots = jnp.where(filled > 0, slot_total, region_slots).astype(BF16)
    outgoing = jnp.concatenate(
        [outgoing, jnp.broadcast_to(out_slots[:, None], (capacity_all, LANES))], axis=1
    )
    incoming = lax.all_to_all(
        outgoing.reshape(count_all, capacity, row_width + LANES),
        ("rx", "ry"),
        split_axis=0,
        concat_axis=0,
        tiled=True,
    ).reshape(capacity_all, row_width + LANES)
    in_slots = incoming[:, row_width].astype(jnp.int32)

    cot_rows = cotangent.reshape(region_slots, row_width)
    planes = pltpu.VMEM((3, region_x + 2, region_y + 2, depth, LANES), BF16)
    table = pltpu.VMEM((36 * LANES, 2 * LANES), BF16)
    voxels = region_slots * depth
    padded = -(-(54 * channels * channels // LANES) // (16 * count_all)) * 16 * count_all
    share = padded // count_all
    factor = float(1.0 / (count_all * shard_rows * depth) ** 0.5)
    row_shape = jax.ShapeDtypeStruct((region_slots, row_width), BF16)
    grad_shape = jax.ShapeDtypeStruct((27, channels, channels), F32)
    out_rows, back_rows, first_grad, second_grad = pl.pallas_call(
        functools.partial(core_kernel, count_x, count_y, factor),
        out_shape=(
            row_shape,
            jax.ShapeDtypeStruct((capacity_all, row_width), BF16),
            grad_shape,
            grad_shape,
        ),
        in_specs=[pl.BlockSpec(memory_space=pltpu.VMEM)] * 6,
        out_specs=[pl.BlockSpec(memory_space=pltpu.VMEM)] * 4,
        scratch_shapes=[
            planes, planes, planes, planes,
            table, table, table, table,
            pltpu.VMEM((row_width, depth * LANES), BF16),
            pltpu.VMEM((voxels, LANES), F32),
            pltpu.VMEM((voxels, LANES), F32),
            pltpu.VMEM((voxels, LANES), F32),
            pltpu.VMEM((2 * LANES, voxels // 2), BF16),
            pltpu.VMEM((45, LANES, LANES), F32),
            pltpu.VMEM((padded, LANES), F32),
            pltpu.VMEM((count_all, share, LANES), BF16),
            pltpu.VMEM((count_all - 1, share, LANES), BF16),
            pltpu.VMEM((count_all, share, LANES), BF16),
            pltpu.SemaphoreType.DMA((4, len(SIDES))),
            pltpu.SemaphoreType.DMA((4, len(SIDES))),
            pltpu.SemaphoreType.DMA((2,)),
            pltpu.SemaphoreType.DMA((2,)),
        ],
        compiler_params=pltpu.CompilerParams(
            vmem_limit_bytes=VMEM_LIMIT, collective_id=1, has_side_effects=True
        ),
    )(
        incoming, in_slots[None, :], in_slots[:, None], cot_rows, first_weight, second_weight
    )
    returned = lax.all_to_all(
        back_rows.reshape(count_all, capacity, row_width),
        ("rx", "ry"),
        split_axis=0,
        concat_axis=0,
        tiled=True,
    ).reshape(capacity_all, row_width)
    feature_grads = jnp.dot(send_table, returned, preferred_element_type=F32).astype(BF16)
    return (
        out_rows.reshape(region_x, region_y, row_width),
        feature_grads,
        first_grad,
        second_grad,
    )


def solution(mesh):
    in_specs = (P(("rx", "ry"), None), P(("rx", "ry")), P("rx", "ry", None), P(), P())
    out_specs = (P("rx", "ry", None), P(("rx", "ry"), None), P(), P())
    return jax.shard_map(
        on_device, mesh=mesh, in_specs=in_specs, out_specs=out_specs, check_vma=False
    )
```

```python
import functools

import jax
import jax.numpy as jnp
from jax import lax
from jax.experimental import pallas as pl
from jax.experimental.pallas import tpu as pltpu
from jax.sharding import PartitionSpec as P

F32 = jnp.float32
BF16 = jnp.bfloat16
LANES = 128
VMEM_LIMIT = 64 * 1024 * 1024 - 64 * 1024
SIDES = [(dx, dy) for dx in (-1, 0, 1) for dy in (-1, 0, 1) if (dx, dy) != (0, 0)]


def params():
    return pltpu.CompilerParams(vmem_limit_bytes=VMEM_LIMIT)


def iota(shape, dim):
    return lax.broadcasted_iota(jnp.int32, shape, dim)


def build_move(move, depth):
    width = move.shape[0]
    k = iota((width, 2 * LANES), 0)
    n = iota((width, 2 * LANES), 1)
    base = k - (n % LANES) * depth - n // LANES
    for zp in range(depth // 2):
        move[:, zp * 2 * LANES : (zp + 1) * 2 * LANES] = jnp.where(
            base == 2 * zp, 1.0, 0.0
        ).astype(BF16)


def spread_columns(rows, scale, move, scratch, depth):
    count = rows.shape[0]
    for zp in range(depth // 2):
        moved = jnp.dot(
            rows, move[:, zp * 2 * LANES : (zp + 1) * 2 * LANES], preferred_element_type=F32
        )
        if scale is not None:
            moved = moved * scale
        scratch[pl.ds(2 * zp, count, stride=depth), :] = moved[:, :LANES]
        scratch[pl.ds(2 * zp + 1, count, stride=depth), :] = moved[:, LANES:]


def gather_columns(scratch, move, count, depth):
    wide = jnp.concatenate(
        [scratch[pl.ds(z, count, stride=depth), :] for z in range(depth)], axis=1
    ).astype(BF16)
    return lax.dot_general(
        wide, move[...], (((1,), (1,)), ((), ())), preferred_element_type=F32
    ).astype(BF16)


def shift_block(planes, xs, ys):
    block = planes[1, xs, ys]
    count_x, count_y, depth, lanes = block.shape
    total = count_x * count_y * depth
    z = iota((total, lanes), 0) % depth
    v = block.astype(F32).reshape(total, lanes)
    below = jnp.where(z == 0, 0.0, pltpu.roll(v, 1, 0))
    above = jnp.where(z == depth - 1, 0.0, pltpu.roll(v, total - 1, 0))
    planes[0, xs, ys] = below.astype(BF16).reshape(block.shape)
    planes[2, xs, ys] = above.astype(BF16).reshape(block.shape)


def shift_inside(planes):
    rows, columns = planes.shape[1] - 2, planes.shape[2] - 2

    def body(x, carry):
        shift_block(planes, pl.ds(x + 1, 1), pl.ds(1, columns))
        return carry

    lax.fori_loop(0, rows, body, 0)


def shift_border(planes):
    rows, columns = planes.shape[1] - 2, planes.shape[2] - 2
    shift_block(planes, pl.ds(0, 1), pl.ds(0, columns + 2))
    shift_block(planes, pl.ds(rows + 1, 1), pl.ds(0, columns + 2))
    shift_block(planes, pl.ds(1, rows), pl.ds(0, 1))
    shift_block(planes, pl.ds(1, rows), pl.ds(columns + 1, 1))


def clear_border(planes):
    _, count_x, count_y, depth, lanes = planes.shape
    planes[1, 0] = jnp.zeros((count_y, depth, lanes), BF16)
    planes[1, count_x - 1] = jnp.zeros((count_y, depth, lanes), BF16)
    planes[1, :, 0] = jnp.zeros((count_x, depth, lanes), BF16)
    planes[1, :, count_y - 1] = jnp.zeros((count_x, depth, lanes), BF16)


def pair_weights(weights, table, transposed):
    channels = weights.shape[1]
    table[...] = jnp.zeros(table.shape, BF16)
    for a in range(3):
        for b in range(3):
            for c in range(3):
                tap = 9 * a + 3 * b + c
                if transposed:
                    block = weights[tap].astype(F32).T.astype(BF16)
                else:
                    block = weights[26 - tap]
                for p in range(2):
                    row = ((a + p) * 9 + 3 * b + c) * LANES
                    table[row : row + channels, p * LANES : p * LANES + channels] = block


def pair_conv(planes, table, xp, count_y):
    depth = planes.shape[3]
    pieces = []
    for j in range(4):
        for b in range(3):
            for c in range(3):
                pieces.append(
                    planes[c, 2 * xp + j, b : b + count_y].reshape(count_y * depth, LANES)
                )
    return jnp.dot(jnp.concatenate(pieces, axis=1), table[...], preferred_element_type=F32)


def correlate(local, planes, turned, out):
    _, count_x, count_y, depth, _ = local.shape
    count_x, count_y = count_x - 2, count_y - 2
    rows = count_y * depth
    for xp in range(count_x // 2):
        pair = jnp.concatenate(
            [
                local[1, 2 * xp + 1, 1 : count_y + 1].reshape(rows, LANES),
                local[1, 2 * xp + 2, 1 : count_y + 1].reshape(rows, LANES),
            ],
            axis=1,
        )
        turned[:, xp * rows : (xp + 1) * rows] = pair.astype(F32).T.astype(BF16)
    out[...] = jnp.zeros(out.shape, F32)

    def body(step, carry):
        jj = (step // 3) * 2
        b = step % 3
        pieces = []
        for dj in range(2):
            for c in range(3):
                pieces.append(
                    jnp.concatenate(
                        [
                            planes[c, 2 * xp + jj + dj, pl.ds(b, count_y)].reshape(rows, LANES)
                            for xp in range(count_x // 2)
                        ],
                        axis=0,
                    )
                )
        for half in range(3):
            both = jnp.concatenate([pieces[2 * half], pieces[2 * half + 1]], axis=1)
            prod = jnp.dot(turned[...], both, preferred_element_type=F32)
            for s in range(2):
                dj, c = divmod(2 * half + s, 3)
                for p in range(2):
                    slot = (jj + dj - p + 1) * 9 + 3 * b + c
                    out[slot] += prod[p * LANES : (p + 1) * LANES, s * LANES : (s + 1) * LANES]
        return carry

    lax.fori_loop(0, 6, body, 0)


def pack_grads(out, packed, base, flip, channels):
    tall = channels * channels // LANES
    rest = channels - tall
    lane = iota((tall, LANES), 1)

    def body(k, carry):
        block = out[9 + 26 - k].T if flip else out[9 + k]
        low = block[tall:channels]
        part = LANES - channels
        moved = jnp.concatenate(
            [pltpu.roll(low, channels - part * m, 1) for m in range(tall // rest)], axis=0
        )
        at = pl.ds(pl.multiple_of((base + k) * tall, 8), tall)
        packed[at, :] = jnp.where(lane < channels, block[:tall], moved)
        return carry

    lax.fori_loop(0, 27, body, 0)


def unpack_grads(packed, dest, base, factor, channels):
    tall = channels * channels // LANES
    rest = channels - tall
    part = LANES - channels
    lane = iota((rest, LANES), 1)

    def body(k, carry):
        v = packed[pl.ds(pl.multiple_of((base + k) * tall, 8), tall), :] * factor
        low = jnp.zeros((rest, LANES), F32)
        for m in range(tall // rest):
            turned = pltpu.roll(v[m * rest : (m + 1) * rest], (part * m - channels) % LANES, 1)
            low = jnp.where(lane // part == m, turned, low)
        dest[k, :tall, :] = v[:, :channels]
        dest[k, tall:, :] = low[:, :channels]
        return carry

    lax.fori_loop(0, 27, body, 0)


class Halo:
    def __init__(self, planes, send_sem, recv_sem, grid):
        self.planes, self.send_sem, self.recv_sem, self.grid = planes, send_sem, recv_sem, grid
        self.extent = (planes.shape[1] - 2, planes.shape[2] - 2)

    def copy(self, k):
        source, target = [], []
        for step, extent in zip(SIDES[k], self.extent):
            source.append({0: pl.ds(1, extent), 1: pl.ds(extent, 1), -1: pl.ds(1, 1)}[step])
            target.append({0: pl.ds(1, extent), 1: pl.ds(0, 1), -1: pl.ds(extent + 1, 1)}[step])
        (ix, iy, _, _), (dx, dy) = self.grid, SIDES[k]
        return pltpu.make_async_remote_copy(
            src_ref=self.planes.at[1, source[0], source[1]],
            dst_ref=self.planes.at[1, target[0], target[1]],
            send_sem=self.send_sem.at[k],
            recv_sem=self.recv_sem.at[k],
            device_id=(ix + dx, iy + dy),
            device_id_type=pl.DeviceIdType.MESH,
        )

    def there(self, dx, dy):
        ix, iy, nx, ny = self.grid
        return jnp.logical_and(
            jnp.logical_and(ix + dx >= 0, ix + dx < nx), jnp.logical_and(iy + dy >= 0, iy + dy < ny)
        )

    def start(self):
        for k, (dx, dy) in enumerate(SIDES):

            @pl.when(self.there(dx, dy))
            def _():
                self.copy(k).start()

    def wait(self):
        for k, (dx, dy) in enumerate(SIDES):

            @pl.when(self.there(-dx, -dy))
            def _():
                self.copy(k).wait_recv()

            @pl.when(self.there(dx, dy))
            def _():
                self.copy(k).wait_send()


def lay_messages(parts, scratch, dest):
    devices, height, _ = dest.shape
    pitch = scratch.shape[0] // devices
    for row, value in enumerate(parts):
        scratch[pl.ds(row, devices, stride=pitch), :] = value
    flat = scratch[...].reshape(devices, pitch, LANES)
    dest[...] = flat[:, :height].astype(BF16)


def read_messages(source, scratch, capacity):
    devices, height, _ = source.shape
    pitch = scratch.shape[0] // devices
    each = height // capacity
    filler = jnp.zeros((devices, pitch - height, LANES), F32)
    scratch[...] = jnp.concatenate([source[...].astype(F32), filler], axis=1).reshape(
        scratch.shape
    )
    return jnp.concatenate(
        [
            jnp.concatenate(
                [
                    scratch[pl.ds(k * each + j, devices, stride=pitch), :].astype(BF16)
                    for j in range(each)
                ],
                axis=1,
            )
            for k in range(capacity)
        ],
        axis=0,
    )


def core_kernel(
    nx, ny, capacity, factor,
    feat_ref, route_row_ref, route_col_ref, cot_ref, w1_ref, w2_ref,
    out_ref, fg_ref, dw1_ref, dw2_ref,
    x3, g3, a3, h3, tx, tg, ta, th, move, s1, s2, mask_p, turned, grads,
    packed, shares, spread, whole,
    sent, got, back_sent, back_got, routes,
    halo_send, halo_recv, sum_send, sum_recv, col_send, col_recv,
):
    ix, iy = lax.axis_index("rx"), lax.axis_index("ry")
    count = nx * ny
    me = ix * ny + iy
    barrier = pltpu.get_barrier_semaphore()
    mesh_id = pl.DeviceIdType.MESH

    def peer(d):
        other = lax.rem(me + d, count)
        return (lax.div(other, ny), lax.rem(other, ny))

    for planes in (x3, g3, a3, h3):
        clear_border(planes)

    def greet(d, carry):
        pl.semaphore_signal(barrier, inc=1, device_id=peer(d), device_id_type=mesh_id)
        return carry

    lax.fori_loop(1, count, greet, 0)
    _, count_x, count_y, depth, _ = x3.shape
    count_x, count_y = count_x - 2, count_y - 2
    rows = count_y * depth
    slots, width = cot_ref.shape
    shard = feat_ref.shape[0]
    channels = w1_ref.shape[1]
    grid = (ix, iy, nx, ny)
    halos = [
        Halo(planes, halo_send.at[k], halo_recv.at[k], grid)
        for k, planes in enumerate((x3, g3, a3, h3))
    ]
    inside = (pl.ds(1, count_x), pl.ds(1, count_y))

    row, col = route_row_ref[...], route_col_ref[...]
    owner_row, owner_col = lax.div(row, slots), lax.div(col, slots)
    same = owner_col == owner_row
    s0, s1_ = iota((shard, shard), 0), iota((shard, shard), 1)
    rank_row = jnp.sum(jnp.where(same & (s0 < s1_), 1.0, 0.0), axis=0, keepdims=True)
    rank_col = jnp.sum(jnp.where(same & (s1_ < s0), 1.0, 0.0), axis=1, keepdims=True)
    ahead_row = lax.rem(owner_row - me + count, count)
    ahead_col = lax.rem(owner_col - me + count, count)
    place_row = rank_row.astype(jnp.int32) * count + ahead_row
    place_col = rank_col.astype(jnp.int32) * count + ahead_col
    buffer = capacity * count
    send_hot = jnp.where(iota((buffer, shard), 0) == place_row, 1.0, 0.0).astype(BF16)
    return_hot = jnp.where(iota((shard, buffer), 1) == place_col, 1.0, 0.0).astype(BF16)
    outgoing = jnp.dot(send_hot, feat_ref[...], preferred_element_type=F32)
    lay_messages(
        [
            outgoing[k * count : (k + 1) * count, j * LANES : (j + 1) * LANES]
            for k in range(capacity)
            for j in range(width // LANES)
        ],
        s1,
        sent,
    )
    routes[0] = row
    got[0] = sent[0]
    pl.semaphore_wait(barrier, count - 1)

    def send_route(d, carry):
        pltpu.make_async_remote_copy(
            src_ref=route_row_ref,
            dst_ref=routes.at[d],
            send_sem=col_send.at[0],
            recv_sem=col_recv.at[0],
            device_id=peer(d),
            device_id_type=mesh_id,
        ).start()
        return carry

    def send_column(d, carry):
        pltpu.make_async_remote_copy(
            src_ref=sent.at[d],
            dst_ref=got.at[d],
            send_sem=col_send.at[1],
            recv_sem=col_recv.at[1],
            device_id=peer(d),
            device_id_type=mesh_id,
        ).start()
        return carry

    def wait_all(ref, sem):
        pltpu.make_async_copy(ref.at[pl.ds(1, count - 1)], ref.at[pl.ds(1, count - 1)], sem).wait()

    lax.fori_loop(1, count, send_route, 0)
    lax.fori_loop(1, count, send_column, 0)

    build_move(move, depth)
    spread_columns(cot_ref[...], None, move, s2, depth)
    pair_weights(w2_ref, tg, False)
    wait_all(routes, col_recv.at[0])

    known = routes[...].reshape(count, shard)
    mine = lax.div(known, slots) == me
    mine_f = jnp.where(mine, 1.0, 0.0)
    upper = jnp.where(s0 < s1_, 1.0, 0.0).astype(BF16)
    before = jnp.dot(mine_f.astype(BF16), upper, preferred_element_type=F32)
    slot_of = lax.rem(known, slots).astype(F32)
    slot_cols, slot_rows = [], []
    for k in range(capacity):
        chosen = mine & (before == float(k))
        found = jnp.sum(jnp.where(chosen, slot_of + 1.0, 0.0), axis=1, keepdims=True) - 1.0
        slot_cols.append(found)
        slot_rows.append(jnp.broadcast_to(found, (count, LANES)).T[:1, :])
    slot_row = jnp.concatenate(slot_rows, axis=1).astype(jnp.int32)
    slot_col = jnp.concatenate(slot_cols, axis=0).astype(jnp.int32)
    hot = jnp.where(slot_row == iota((slots, buffer), 0), 1.0, 0.0)
    back_hot = jnp.where(slot_col == iota((buffer, slots), 1), 1.0, 0.0).astype(BF16)
    active = jnp.sum(hot, axis=1, keepdims=True)
    wide = jnp.broadcast_to(active, (slots, LANES))
    for z in range(depth):
        mask_p[pl.ds(z, slots, stride=depth), :] = wide
    g3[1, inside[0], inside[1]] = (
        (s2[...] * mask_p[...]).astype(BF16).reshape(count_x, count_y, depth, LANES)
    )
    halos[1].start()
    shift_inside(g3)
    pair_weights(w1_ref, tx, True)
    pair_weights(w2_ref, ta, True)
    pair_weights(w1_ref, th, False)
    halos[1].wait()
    shift_border(g3)

    wait_all(got, col_recv.at[1])
    arrived = read_messages(got, s1, capacity)
    field_rows = jnp.dot(hot.astype(BF16), arrived, preferred_element_type=F32).astype(BF16)
    spread_columns(field_rows, None, move, s1, depth)
    x3[1, inside[0], inside[1]] = s1[...].astype(BF16).reshape(count_x, count_y, depth, LANES)
    halos[0].start()
    shift_inside(x3)

    def conv_to(planes, table, dest):
        def body(xp, carry):
            both = pair_conv(planes, table, xp, count_y)
            for p in range(2):
                at = pl.ds(pl.multiple_of((2 * xp + p) * rows, rows), rows)
                dest[at, :] = both[:, p * LANES : (p + 1) * LANES]
            return carry

        lax.fori_loop(0, count_x // 2, body, 0)

    conv_to(g3, tg, s2)
    halos[0].wait()
    shift_border(x3)

    def forward(xp, carry):
        hidden2 = pair_conv(x3, tx, xp, count_y)
        for p in range(2):
            x = 2 * xp + p
            at = pl.ds(pl.multiple_of(x * rows, rows), rows)
            mask = mask_p[at, :]
            hidden = mask * hidden2[:, p * LANES : (p + 1) * LANES]
            s = 1.0 / (1.0 + jnp.exp(-hidden))
            a3[1, x + 1, 1 : count_y + 1] = (
                (hidden * s).astype(BF16).reshape(count_y, depth, LANES)
            )
            hg = mask * s2[at, :] * s * (1.0 + hidden * (1.0 - s))
            h3[1, x + 1, 1 : count_y + 1] = hg.astype(BF16).reshape(count_y, depth, LANES)
        return carry

    lax.fori_loop(0, count_x // 2, forward, 0)
    halos[3].start()
    halos[2].start()
    used = 27 * channels * channels // LANES
    packed[used:, :] = jnp.zeros((packed.shape[0] - used, LANES), F32)

    def sum_out(half, local, planes, flip):
        correlate(local, planes, turned, grads)
        pack_grads(grads, packed, 0, flip, channels)
        shares[half] = packed[...].astype(BF16).reshape(shares.shape[1:])

        def send_share(d, carry):
            other = lax.rem(me + d, count)
            pltpu.make_async_remote_copy(
                src_ref=shares.at[half, other],
                dst_ref=spread.at[half, d],
                send_sem=sum_send.at[half],
                recv_sem=sum_recv.at[half],
                device_id=peer(d),
                device_id_type=mesh_id,
            ).start()
            return carry

        lax.fori_loop(1, count, send_share, 0)

    sum_out(0, h3, x3, False)
    sum_out(1, a3, g3, True)
    shift_inside(h3)
    shift_inside(a3)
    halos[3].wait()
    shift_border(h3)

    def grad_body(xp, carry):
        both = pair_conv(h3, th, xp, count_y)
        for p in range(2):
            x = 2 * xp + p
            at = pl.ds(pl.multiple_of(x * rows, rows), rows)
            cot = g3[1, x + 1, 1 : count_y + 1].reshape(rows, LANES).astype(F32)
            s2[at, :] = cot + both[:, p * LANES : (p + 1) * LANES]
        return carry

    lax.fori_loop(0, count_x // 2, grad_body, 0)
    grad_rows = gather_columns(s2, move, slots, depth)
    back_rows = jnp.dot(back_hot, grad_rows, preferred_element_type=F32)
    lay_messages(
        [
            back_rows[k * count : (k + 1) * count, j * LANES : (j + 1) * LANES]
            for k in range(capacity)
            for j in range(width // LANES)
        ],
        s1,
        back_sent,
    )
    back_got[0] = back_sent[0]

    def send_back(d, carry):
        pltpu.make_async_remote_copy(
            src_ref=back_sent.at[d],
            dst_ref=back_got.at[d],
            send_sem=col_send.at[2],
            recv_sem=col_recv.at[2],
            device_id=peer(count - d),
            device_id_type=mesh_id,
        ).start()
        return carry

    lax.fori_loop(1, count, send_back, 0)

    for half in range(2):
        wait_all(spread.at[half], sum_recv.at[half])
        own_share = shares[half, me].astype(F32)
        total = lax.fori_loop(
            1, count, lambda d, acc: acc + spread[half, d].astype(F32), own_share
        )
        whole[half, me] = total.astype(BF16)

        def send_total(d, carry):
            pltpu.make_async_remote_copy(
                src_ref=whole.at[half, me],
                dst_ref=whole.at[half, me],
                send_sem=sum_send.at[2 + half],
                recv_sem=sum_recv.at[2 + half],
                device_id=peer(d),
                device_id_type=mesh_id,
            ).start()
            return carry

        lax.fori_loop(1, count, send_total, 0)

    halos[2].wait()
    shift_border(a3)

    def block_body(xp, carry):
        both = pair_conv(a3, ta, xp, count_y)
        for p in range(2):
            x = 2 * xp + p
            at = pl.ds(pl.multiple_of(x * rows, rows), rows)
            own = x3[1, x + 1, 1 : count_y + 1].reshape(rows, LANES).astype(F32)
            s1[at, :] = own + mask_p[at, :] * both[:, p * LANES : (p + 1) * LANES]
        return carry

    lax.fori_loop(0, count_x // 2, block_body, 0)
    out_ref[...] = gather_columns(s1, move, slots, depth)

    wait_all(back_got, col_recv.at[2])
    returned = read_messages(back_got, s2, capacity)
    fg_ref[...] = jnp.dot(return_hot, returned, preferred_element_type=F32).astype(BF16)

    for half, dest in enumerate((dw1_ref, dw2_ref)):
        wait_all(whole.at[half], sum_recv.at[2 + half])
        packed[...] = whole[half].astype(F32).reshape(packed.shape)
        unpack_grads(packed, dest, 0, factor, channels)
    wait_all(routes, col_send.at[0])
    wait_all(got, col_send.at[1])
    wait_all(back_got, col_send.at[2])
    for half in range(2):
        wait_all(spread.at[half], sum_send.at[half])
        wait_all(whole.at[half], sum_send.at[2 + half])


def on_device(column_features, column_route, cotangent, first_weight, second_weight):
    count_x = lax.axis_size("rx")
    count_y = lax.axis_size("ry")
    count_all = count_x * count_y
    shard_rows, row_width = column_features.shape
    region_x, region_y = cotangent.shape[:2]
    channels = first_weight.shape[1]
    depth = row_width // channels
    region_slots = region_x * region_y
    capacity = 2 * shard_rows // count_all
    planes = pltpu.VMEM((3, region_x + 2, region_y + 2, depth, LANES), BF16)
    table = pltpu.VMEM((36 * LANES, 2 * LANES), BF16)
    voxels = region_slots * depth
    flat = pltpu.VMEM((voxels, LANES), F32)
    padded = -(-(27 * channels * channels // LANES) // (16 * count_all)) * 16 * count_all
    share = pltpu.VMEM((2, count_all, padded // count_all, LANES), BF16)
    messages = pltpu.VMEM((count_all, capacity * row_width // LANES, LANES), BF16)
    factor = float(1.0 / (count_all * shard_rows * depth) ** 0.5)
    grad_shape = jax.ShapeDtypeStruct((27, channels, channels), F32)
    out_rows, feature_grads, first_grad, second_grad = pl.pallas_call(
        functools.partial(core_kernel, count_x, count_y, capacity, factor),
        out_shape=(
            jax.ShapeDtypeStruct((region_slots, row_width), BF16),
            jax.ShapeDtypeStruct((shard_rows, row_width), BF16),
            grad_shape,
            grad_shape,
        ),
        in_specs=[pl.BlockSpec(memory_space=pltpu.VMEM)] * 6,
        out_specs=[pl.BlockSpec(memory_space=pltpu.VMEM)] * 4,
        scratch_shapes=[
            planes, planes, planes, planes,
            table, table, table, table,
            pltpu.VMEM((row_width, depth * LANES), BF16),
            flat, flat, flat,
            pltpu.VMEM((2 * LANES, voxels // 2), BF16),
            pltpu.VMEM((45, LANES, LANES), F32),
            pltpu.VMEM((padded, LANES), F32),
            share, share, share,
            messages, messages, messages, messages,
            pltpu.VMEM((count_all, 1, shard_rows), jnp.int32),
            pltpu.SemaphoreType.DMA((4, len(SIDES))),
            pltpu.SemaphoreType.DMA((4, len(SIDES))),
            pltpu.SemaphoreType.DMA((4,)),
            pltpu.SemaphoreType.DMA((4,)),
            pltpu.SemaphoreType.DMA((3,)),
            pltpu.SemaphoreType.DMA((3,)),
        ],
        compiler_params=pltpu.CompilerParams(
            vmem_limit_bytes=VMEM_LIMIT, collective_id=1, has_side_effects=True
        ),
    )(
        column_features,
        column_route[None, :],
        column_route[:, None],
        cotangent.reshape(region_slots, row_width),
        first_weight,
        second_weight,
    )
    return (
        out_rows.reshape(region_x, region_y, row_width),
        feature_grads,
        first_grad,
        second_grad,
    )


def solution(mesh):
    in_specs = (P(("rx", "ry"), None), P(("rx", "ry")), P("rx", "ry", None), P(), P())
    out_specs = (P("rx", "ry", None), P(("rx", "ry"), None), P(), P())
    return jax.shard_map(
        on_device, mesh=mesh, in_specs=in_specs, out_specs=out_specs, check_vma=False
    )
```

```python
import functools

import jax
import jax.numpy as jnp
from jax import lax
from jax.experimental import pallas as pl
from jax.experimental.pallas import tpu as pltpu
from jax.sharding import PartitionSpec as P

F32 = jnp.float32
BF16 = jnp.bfloat16
LANES = 128
VMEM_LIMIT = 64 * 1024 * 1024 - 64 * 1024
SIDES = [(dx, dy) for dx in (-1, 0, 1) for dy in (-1, 0, 1) if (dx, dy) != (0, 0)]


def params():
    return pltpu.CompilerParams(vmem_limit_bytes=VMEM_LIMIT)


def iota(shape, dim):
    return lax.broadcasted_iota(jnp.int32, shape, dim)


def build_move(move, depth):
    width = move.shape[0]
    k = iota((width, 2 * LANES), 0)
    n = iota((width, 2 * LANES), 1)
    base = k - (n % LANES) * depth - n // LANES
    for zp in range(depth // 2):
        move[:, zp * 2 * LANES : (zp + 1) * 2 * LANES] = jnp.where(
            base == 2 * zp, 1.0, 0.0
        ).astype(BF16)


def spread_columns(rows, scale, move, scratch, depth):
    count = rows.shape[0]
    for zp in range(depth // 2):
        moved = jnp.dot(
            rows, move[:, zp * 2 * LANES : (zp + 1) * 2 * LANES], preferred_element_type=F32
        )
        if scale is not None:
            moved = moved * scale
        scratch[pl.ds(2 * zp, count, stride=depth), :] = moved[:, :LANES]
        scratch[pl.ds(2 * zp + 1, count, stride=depth), :] = moved[:, LANES:]


def gather_columns(scratch, move, count, depth):
    wide = jnp.concatenate(
        [scratch[pl.ds(z, count, stride=depth), :] for z in range(depth)], axis=1
    ).astype(BF16)
    return lax.dot_general(
        wide, move[...], (((1,), (1,)), ((), ())), preferred_element_type=F32
    ).astype(BF16)


def shift_block(planes, xs, ys):
    block = planes[1, xs, ys]
    count_x, count_y, depth, lanes = block.shape
    total = count_x * count_y * depth
    z = iota((total, lanes), 0) % depth
    v = block.astype(F32).reshape(total, lanes)
    below = jnp.where(z == 0, 0.0, pltpu.roll(v, 1, 0))
    above = jnp.where(z == depth - 1, 0.0, pltpu.roll(v, total - 1, 0))
    planes[0, xs, ys] = below.astype(BF16).reshape(block.shape)
    planes[2, xs, ys] = above.astype(BF16).reshape(block.shape)


def shift_inside(planes):
    rows, columns = planes.shape[1] - 2, planes.shape[2] - 2

    def body(x, carry):
        shift_block(planes, pl.ds(x + 1, 1), pl.ds(1, columns))
        return carry

    lax.fori_loop(0, rows, body, 0)


def shift_border(planes):
    rows, columns = planes.shape[1] - 2, planes.shape[2] - 2
    shift_block(planes, pl.ds(0, 1), pl.ds(0, columns + 2))
    shift_block(planes, pl.ds(rows + 1, 1), pl.ds(0, columns + 2))
    shift_block(planes, pl.ds(1, rows), pl.ds(0, 1))
    shift_block(planes, pl.ds(1, rows), pl.ds(columns + 1, 1))


def clear_border(planes):
    _, count_x, count_y, depth, lanes = planes.shape
    planes[1, 0] = jnp.zeros((count_y, depth, lanes), BF16)
    planes[1, count_x - 1] = jnp.zeros((count_y, depth, lanes), BF16)
    planes[1, :, 0] = jnp.zeros((count_x, depth, lanes), BF16)
    planes[1, :, count_y - 1] = jnp.zeros((count_x, depth, lanes), BF16)


def pair_weights(weights, table, transposed):
    channels = weights.shape[1]
    table[...] = jnp.zeros(table.shape, BF16)
    for a in range(3):
        for b in range(3):
            for c in range(3):
                tap = 9 * a + 3 * b + c
                if transposed:
                    block = weights[tap].astype(F32).T.astype(BF16)
                else:
                    block = weights[26 - tap]
                for p in range(2):
                    row = ((a + p) * 9 + 3 * b + c) * LANES
                    table[row : row + channels, p * LANES : p * LANES + channels] = block


def pair_conv(planes, table, xp, count_y):
    depth = planes.shape[3]
    pieces = []
    for j in range(4):
        for b in range(3):
            for c in range(3):
                pieces.append(
                    planes[c, 2 * xp + j, b : b + count_y].reshape(count_y * depth, LANES)
                )
    return jnp.dot(jnp.concatenate(pieces, axis=1), table[...], preferred_element_type=F32)


def correlate(local, planes, turned, out):
    _, count_x, count_y, depth, _ = local.shape
    count_x, count_y = count_x - 2, count_y - 2
    rows = count_y * depth
    for xp in range(count_x // 2):
        pair = jnp.concatenate(
            [
                local[1, 2 * xp + 1, 1 : count_y + 1].reshape(rows, LANES),
                local[1, 2 * xp + 2, 1 : count_y + 1].reshape(rows, LANES),
            ],
            axis=1,
        )
        turned[:, xp * rows : (xp + 1) * rows] = pair.astype(F32).T.astype(BF16)
    out[...] = jnp.zeros(out.shape, F32)

    def body(step, carry):
        jj = (step // 3) * 2
        b = step % 3
        pieces = []
        for dj in range(2):
            for c in range(3):
                pieces.append(
                    jnp.concatenate(
                        [
                            planes[c, 2 * xp + jj + dj, pl.ds(b, count_y)].reshape(rows, LANES)
                            for xp in range(count_x // 2)
                        ],
                        axis=0,
                    )
                )
        for half in range(3):
            both = jnp.concatenate([pieces[2 * half], pieces[2 * half + 1]], axis=1)
            prod = jnp.dot(turned[...], both, preferred_element_type=F32)
            for s in range(2):
                dj, c = divmod(2 * half + s, 3)
                for p in range(2):
                    slot = (jj + dj - p + 1) * 9 + 3 * b + c
                    out[slot] += prod[p * LANES : (p + 1) * LANES, s * LANES : (s + 1) * LANES]
        return carry

    lax.fori_loop(0, 6, body, 0)


def pack_grads(out, packed, base, flip, channels):
    tall = channels * channels // LANES
    rest = channels - tall
    lane = iota((tall, LANES), 1)

    def body(k, carry):
        block = out[9 + 26 - k].T if flip else out[9 + k]
        low = block[tall:channels]
        part = LANES - channels
        moved = jnp.concatenate(
            [pltpu.roll(low, channels - part * m, 1) for m in range(tall // rest)], axis=0
        )
        at = pl.ds(pl.multiple_of((base + k) * tall, 8), tall)
        packed[at, :] = jnp.where(lane < channels, block[:tall], moved)
        return carry

    lax.fori_loop(0, 27, body, 0)


def unpack_grads(packed, dest, base, factor, channels):
    tall = channels * channels // LANES
    rest = channels - tall
    part = LANES - channels
    lane = iota((rest, LANES), 1)

    def body(k, carry):
        v = packed[pl.ds(pl.multiple_of((base + k) * tall, 8), tall), :] * factor
        low = jnp.zeros((rest, LANES), F32)
        for m in range(tall // rest):
            turned = pltpu.roll(v[m * rest : (m + 1) * rest], (part * m - channels) % LANES, 1)
            low = jnp.where(lane // part == m, turned, low)
        dest[k, :tall, :] = v[:, :channels]
        dest[k, tall:, :] = low[:, :channels]
        return carry

    lax.fori_loop(0, 27, body, 0)


class Halo:
    def __init__(self, planes, send_sem, recv_sem, grid):
        self.planes, self.send_sem, self.recv_sem, self.grid = planes, send_sem, recv_sem, grid
        self.extent = (planes.shape[1] - 2, planes.shape[2] - 2)

    def copy(self, k):
        source, target = [], []
        for step, extent in zip(SIDES[k], self.extent):
            source.append({0: pl.ds(1, extent), 1: pl.ds(extent, 1), -1: pl.ds(1, 1)}[step])
            target.append({0: pl.ds(1, extent), 1: pl.ds(0, 1), -1: pl.ds(extent + 1, 1)}[step])
        (ix, iy, _, _), (dx, dy) = self.grid, SIDES[k]
        return pltpu.make_async_remote_copy(
            src_ref=self.planes.at[1, source[0], source[1]],
            dst_ref=self.planes.at[1, target[0], target[1]],
            send_sem=self.send_sem.at[k],
            recv_sem=self.recv_sem.at[k],
            device_id=(ix + dx, iy + dy),
            device_id_type=pl.DeviceIdType.MESH,
        )

    def there(self, dx, dy):
        ix, iy, nx, ny = self.grid
        return jnp.logical_and(
            jnp.logical_and(ix + dx >= 0, ix + dx < nx), jnp.logical_and(iy + dy >= 0, iy + dy < ny)
        )

    def start(self):
        for k, (dx, dy) in enumerate(SIDES):

            @pl.when(self.there(dx, dy))
            def _():
                self.copy(k).start()

    def wait(self):
        for k, (dx, dy) in enumerate(SIDES):

            @pl.when(self.there(-dx, -dy))
            def _():
                self.copy(k).wait_recv()

            @pl.when(self.there(dx, dy))
            def _():
                self.copy(k).wait_send()


def lay_messages(parts, scratch, dest):
    devices, height, _ = dest.shape
    pitch = scratch.shape[0] // devices
    for row, value in enumerate(parts):
        scratch[pl.ds(row, devices, stride=pitch), :] = value
    flat = scratch[...].reshape(devices, pitch, LANES)
    dest[...] = flat[:, :height].astype(BF16)


def read_messages(source, scratch, capacity):
    devices, height, _ = source.shape
    pitch = scratch.shape[0] // devices
    each = height // capacity
    filler = jnp.zeros((devices, pitch - height, LANES), F32)
    scratch[...] = jnp.concatenate([source[...].astype(F32), filler], axis=1).reshape(
        scratch.shape
    )
    return jnp.concatenate(
        [
            jnp.concatenate(
                [
                    scratch[pl.ds(k * each + j, devices, stride=pitch), :].astype(BF16)
                    for j in range(each)
                ],
                axis=1,
            )
            for k in range(capacity)
        ],
        axis=0,
    )


def core_kernel(
    nx, ny, capacity,
    feat_ref, route_row_ref, cot_ref, w1_ref, w2_ref,
    out_ref, fg_ref, sum_ref,
    x3, g3, a3, h3, tx, tg, ta, th, move, s1, s2, mask_p, turned, grads,
    packed, shares, spread, whole,
    sent, got, back_sent, back_got, routes,
    halo_send, halo_recv, sum_send, sum_recv, pair_send, pair_recv, col_send, col_recv,
):
    ix, iy = lax.axis_index("rx"), lax.axis_index("ry")
    count = nx * ny
    me = ix * ny + iy
    barrier = pltpu.get_barrier_semaphore()
    mesh_id = pl.DeviceIdType.MESH

    def peer(d):
        other = lax.rem(me + d, count)
        return (lax.div(other, ny), lax.rem(other, ny))

    for planes in (x3, g3, a3, h3):
        clear_border(planes)

    def greet(d, carry):
        pl.semaphore_signal(barrier, inc=1, device_id=peer(d), device_id_type=mesh_id)
        return carry

    lax.fori_loop(1, count, greet, 0)
    _, count_x, count_y, depth, _ = x3.shape
    count_x, count_y = count_x - 2, count_y - 2
    rows = count_y * depth
    slots, width = cot_ref.shape
    shard = feat_ref.shape[0]
    channels = w1_ref.shape[1]
    grid = (ix, iy, nx, ny)
    halos = [
        Halo(planes, halo_send.at[k], halo_recv.at[k], grid)
        for k, planes in enumerate((x3, g3, a3, h3))
    ]
    inside = (pl.ds(1, count_x), pl.ds(1, count_y))

    row = route_row_ref[...]
    col = jnp.broadcast_to(row.astype(F32), (shard, shard)).T[:, :1].astype(jnp.int32)
    owner_row, owner_col = lax.div(row, slots), lax.div(col, slots)
    same = owner_col == owner_row
    s0, s1_ = iota((shard, shard), 0), iota((shard, shard), 1)
    rank_row = jnp.sum(jnp.where(same & (s0 < s1_), 1.0, 0.0), axis=0, keepdims=True)
    rank_col = jnp.sum(jnp.where(same & (s1_ < s0), 1.0, 0.0), axis=1, keepdims=True)
    ahead_row = lax.rem(owner_row - me + count, count)
    ahead_col = lax.rem(owner_col - me + count, count)
    place_row = rank_row.astype(jnp.int32) * count + ahead_row
    place_col = rank_col.astype(jnp.int32) * count + ahead_col
    buffer = capacity * count
    send_hot = jnp.where(iota((buffer, shard), 0) == place_row, 1.0, 0.0).astype(BF16)
    return_hot = jnp.where(iota((shard, buffer), 1) == place_col, 1.0, 0.0).astype(BF16)
    outgoing = jnp.dot(send_hot, feat_ref[...], preferred_element_type=F32)
    lay_messages(
        [
            outgoing[k * count : (k + 1) * count, j * LANES : (j + 1) * LANES]
            for k in range(capacity)
            for j in range(width // LANES)
        ],
        s1,
        sent,
    )
    routes[0] = row
    got[0] = sent[0]
    pl.semaphore_wait(barrier, count - 1)

    def send_route(d, carry):
        pltpu.make_async_remote_copy(
            src_ref=route_row_ref,
            dst_ref=routes.at[d],
            send_sem=col_send.at[0],
            recv_sem=col_recv.at[0],
            device_id=peer(d),
            device_id_type=mesh_id,
        ).start()
        return carry

    def send_column(d, carry):
        pltpu.make_async_remote_copy(
            src_ref=sent.at[d],
            dst_ref=got.at[d],
            send_sem=col_send.at[1],
            recv_sem=col_recv.at[1],
            device_id=peer(d),
            device_id_type=mesh_id,
        ).start()
        return carry

    def wait_all(ref, sem):
        pltpu.make_async_copy(ref.at[pl.ds(1, count - 1)], ref.at[pl.ds(1, count - 1)], sem).wait()

    lax.fori_loop(1, count, send_route, 0)
    lax.fori_loop(1, count, send_column, 0)

    build_move(move, depth)
    spread_columns(cot_ref[...], None, move, s2, depth)
    pair_weights(w2_ref, tg, False)
    wait_all(routes, col_recv.at[0])

    known = routes[...].reshape(count, shard)
    mine = lax.div(known, slots) == me
    mine_f = jnp.where(mine, 1.0, 0.0)
    upper = jnp.where(s0 < s1_, 1.0, 0.0).astype(BF16)
    before = jnp.dot(mine_f.astype(BF16), upper, preferred_element_type=F32)
    slot_of = lax.rem(known, slots).astype(F32)
    slot_cols, slot_rows = [], []
    for k in range(capacity):
        chosen = mine & (before == float(k))
        found = jnp.sum(jnp.where(chosen, slot_of + 1.0, 0.0), axis=1, keepdims=True) - 1.0
        slot_cols.append(found)
        slot_rows.append(jnp.broadcast_to(found, (count, LANES)).T[:1, :])
    slot_row = jnp.concatenate(slot_rows, axis=1).astype(jnp.int32)
    slot_col = jnp.concatenate(slot_cols, axis=0).astype(jnp.int32)
    hot = jnp.where(slot_row == iota((slots, buffer), 0), 1.0, 0.0)
    back_hot = jnp.where(slot_col == iota((buffer, slots), 1), 1.0, 0.0).astype(BF16)
    active = jnp.sum(hot, axis=1, keepdims=True)
    wide = jnp.broadcast_to(active, (slots, LANES))
    for z in range(depth):
        mask_p[pl.ds(z, slots, stride=depth), :] = wide
    g3[1, inside[0], inside[1]] = (
        (s2[...] * mask_p[...]).astype(BF16).reshape(count_x, count_y, depth, LANES)
    )
    halos[1].start()
    shift_inside(g3)
    pair_weights(w1_ref, tx, True)
    halos[1].wait()
    shift_border(g3)

    def conv_to(planes, table, dest):
        def body(xp, carry):
            both = pair_conv(planes, table, xp, count_y)
            for p in range(2):
                at = pl.ds(pl.multiple_of((2 * xp + p) * rows, rows), rows)
                dest[at, :] = both[:, p * LANES : (p + 1) * LANES]
            return carry

        lax.fori_loop(0, count_x // 2, body, 0)

    conv_to(g3, tg, s2)
    wait_all(got, col_recv.at[1])
    arrived = read_messages(got, s1, capacity)
    field_rows = jnp.dot(hot.astype(BF16), arrived, preferred_element_type=F32).astype(BF16)
    spread_columns(field_rows, None, move, s1, depth)
    x3[1, inside[0], inside[1]] = s1[...].astype(BF16).reshape(count_x, count_y, depth, LANES)
    halos[0].start()
    shift_inside(x3)
    pair_weights(w2_ref, ta, True)
    pair_weights(w1_ref, th, False)
    halos[0].wait()
    shift_border(x3)

    z_of = iota((rows, LANES), 0) % depth

    def store_shifted(planes, x, v):
        shape = (count_y, depth, LANES)
        below = jnp.where(z_of == 0, 0.0, pltpu.roll(v, 1, 0))
        above = jnp.where(z_of == depth - 1, 0.0, pltpu.roll(v, rows - 1, 0))
        for c, part in enumerate((below, v, above)):
            planes[c, x, 1 : count_y + 1] = part.astype(BF16).reshape(shape)

    def forward(xp, carry):
        hidden2 = pair_conv(x3, tx, xp, count_y)
        for p in range(2):
            x = 2 * xp + p
            at = pl.ds(pl.multiple_of(x * rows, rows), rows)
            mask = mask_p[at, :]
            hidden = mask * hidden2[:, p * LANES : (p + 1) * LANES]
            s = 1.0 / (1.0 + jnp.exp(-hidden))
            store_shifted(a3, x + 1, hidden * s)
            store_shifted(h3, x + 1, mask * s2[at, :] * s * (1.0 + hidden * (1.0 - s)))
        return carry

    lax.fori_loop(0, count_x // 2, forward, 0)
    halos[3].start()
    halos[2].start()
    used = 27 * channels * channels // LANES
    packed[used:, :] = jnp.zeros((packed.shape[0] - used, LANES), F32)
    core, chip = lax.rem(ix, 2), lax.div(ix, 2) * ny + iy
    chips = count // 2

    def share_of(other):
        ox, oy = lax.div(other, ny), lax.rem(other, ny)
        return lax.rem(ox, 2) * chips + lax.div(ox, 2) * ny + oy

    def send_shares(half, local, planes, flip):
        correlate(local, planes, turned, grads)
        pack_grads(grads, packed, 0, flip, channels)
        shares[half] = packed[...].astype(BF16).reshape(shares.shape[1:])

        def send_share(d, carry):
            pltpu.make_async_remote_copy(
                src_ref=shares.at[half, share_of(lax.rem(me + d, count))],
                dst_ref=spread.at[half, d],
                send_sem=sum_send.at[half],
                recv_sem=sum_recv.at[half],
                device_id=peer(d),
                device_id_type=mesh_id,
            ).start()
            return carry

        lax.fori_loop(1, count, send_share, 0)

    def send_totals(half):
        wait_all(spread.at[half], sum_recv.at[half])
        mine = core * chips + chip
        total = lax.fori_loop(
            1,
            count,
            lambda d, acc: acc + spread[half, d].astype(F32),
            shares[half, mine].astype(F32),
        )
        whole[half, mine] = total.astype(BF16)

        def send_total(j, carry):
            other = lax.rem(chip + j, chips)
            pltpu.make_async_remote_copy(
                src_ref=whole.at[half, mine],
                dst_ref=whole.at[half, mine],
                send_sem=sum_send.at[2 + half],
                recv_sem=sum_recv.at[2 + half],
                device_id=(lax.div(other, ny) * 2 + core, lax.rem(other, ny)),
                device_id_type=mesh_id,
            ).start()
            return carry

        lax.fori_loop(1, chips, send_total, 0)

    def across(half):
        mine = whole.at[half, pl.ds(core * chips, chips)]
        return pltpu.make_async_remote_copy(
            src_ref=mine,
            dst_ref=mine,
            send_sem=pair_send.at[half],
            recv_sem=pair_recv.at[half],
            device_id=(ix + 1 - 2 * core, iy),
            device_id_type=mesh_id,
        )

    def wait_same_core(half, sem):
        part = whole.at[half, pl.ds(0, chips - 1)]
        pltpu.make_async_copy(part, part, sem).wait()

    send_shares(0, h3, x3, False)
    halos[3].wait()
    shift_border(h3)

    def grad_body(xp, carry):
        both = pair_conv(h3, th, xp, count_y)
        for p in range(2):
            x = 2 * xp + p
            at = pl.ds(pl.multiple_of(x * rows, rows), rows)
            cot = g3[1, x + 1, 1 : count_y + 1].reshape(rows, LANES).astype(F32)
            s2[at, :] = cot + both[:, p * LANES : (p + 1) * LANES]
        return carry

    lax.fori_loop(0, count_x // 2, grad_body, 0)
    grad_rows = gather_columns(s2, move, slots, depth)
    back_rows = jnp.dot(back_hot, grad_rows, preferred_element_type=F32)
    lay_messages(
        [
            back_rows[k * count : (k + 1) * count, j * LANES : (j + 1) * LANES]
            for k in range(capacity)
            for j in range(width // LANES)
        ],
        s1,
        back_sent,
    )
    back_got[0] = back_sent[0]

    def send_back(d, carry):
        pltpu.make_async_remote_copy(
            src_ref=back_sent.at[d],
            dst_ref=back_got.at[d],
            send_sem=col_send.at[2],
            recv_sem=col_recv.at[2],
            device_id=peer(count - d),
            device_id_type=mesh_id,
        ).start()
        return carry

    lax.fori_loop(1, count, send_back, 0)
    send_shares(1, a3, g3, True)
    send_totals(0)
    halos[2].wait()
    shift_border(a3)

    def block_body(xp, carry):
        both = pair_conv(a3, ta, xp, count_y)
        for p in range(2):
            x = 2 * xp + p
            at = pl.ds(pl.multiple_of(x * rows, rows), rows)
            own = x3[1, x + 1, 1 : count_y + 1].reshape(rows, LANES).astype(F32)
            s1[at, :] = own + mask_p[at, :] * both[:, p * LANES : (p + 1) * LANES]
        return carry

    lax.fori_loop(0, count_x // 2, block_body, 0)
    send_totals(1)
    wait_same_core(0, sum_recv.at[2])
    across(0).start()
    out_ref[...] = gather_columns(s1, move, slots, depth)
    wait_all(back_got, col_recv.at[2])
    returned = read_messages(back_got, s2, capacity)
    fg_ref[...] = jnp.dot(return_hot, returned, preferred_element_type=F32).astype(BF16)
    wait_same_core(1, sum_recv.at[3])
    across(1).start()
    wait_all(routes, col_send.at[0])
    wait_all(got, col_send.at[1])
    wait_all(back_got, col_send.at[2])
    across(0).wait()
    sum_ref[0] = whole[0]
    across(1).wait()
    sum_ref[1] = whole[1]
    for half in range(2):
        wait_all(spread.at[half], sum_send.at[half])
        wait_same_core(half, sum_send.at[2 + half])


def finish_kernel(
    factor, out_in, fg_in, sum_ref, out_ref, fg_ref, dw1_ref, dw2_ref, packed
):
    out_ref[...] = out_in[...].reshape(out_ref.shape)
    fg_ref[...] = fg_in[...]
    channels = dw1_ref.shape[1]
    for half, dest in enumerate((dw1_ref, dw2_ref)):
        packed[...] = sum_ref[half].astype(F32).reshape(packed.shape)
        unpack_grads(packed, dest, 0, factor, channels)


def on_device(column_features, column_route, cotangent, first_weight, second_weight):
    count_x = lax.axis_size("rx")
    count_y = lax.axis_size("ry")
    count_all = count_x * count_y
    shard_rows, row_width = column_features.shape
    region_x, region_y = cotangent.shape[:2]
    channels = first_weight.shape[1]
    depth = row_width // channels
    region_slots = region_x * region_y
    capacity = 2 * shard_rows // count_all
    planes = pltpu.VMEM((3, region_x + 2, region_y + 2, depth, LANES), BF16)
    table = pltpu.VMEM((36 * LANES, 2 * LANES), BF16)
    voxels = region_slots * depth
    flat = pltpu.VMEM((voxels, LANES), F32)
    padded = -(-(27 * channels * channels // LANES) // (16 * count_all)) * 16 * count_all
    share = pltpu.VMEM((2, count_all, padded // count_all, LANES), BF16)
    messages = pltpu.VMEM((count_all, capacity * row_width // LANES, LANES), BF16)
    factor = float(1.0 / (count_all * shard_rows * depth) ** 0.5)
    grad_shape = jax.ShapeDtypeStruct((27, channels, channels), F32)
    vmem = pl.BlockSpec(memory_space=pltpu.VMEM)
    rows_shape = jax.ShapeDtypeStruct((region_slots, row_width), BF16)
    back_shape = jax.ShapeDtypeStruct((shard_rows, row_width), BF16)
    out_rows, back_rows, sums = pl.pallas_call(
        functools.partial(core_kernel, count_x, count_y, capacity),
        out_shape=(
            rows_shape,
            back_shape,
            jax.ShapeDtypeStruct(share.shape, BF16),
        ),
        in_specs=[vmem] * 5,
        out_specs=[vmem] * 3,
        scratch_shapes=[
            planes, planes, planes, planes,
            table, table, table, table,
            pltpu.VMEM((row_width, depth * LANES), BF16),
            flat, flat, flat,
            pltpu.VMEM((2 * LANES, voxels // 2), BF16),
            pltpu.VMEM((45, LANES, LANES), F32),
            pltpu.VMEM((padded, LANES), F32),
            share, share, share,
            messages, messages, messages, messages,
            pltpu.VMEM((count_all, 1, shard_rows), jnp.int32),
            pltpu.SemaphoreType.DMA((4, len(SIDES))),
            pltpu.SemaphoreType.DMA((4, len(SIDES))),
            pltpu.SemaphoreType.DMA((4,)),
            pltpu.SemaphoreType.DMA((4,)),
            pltpu.SemaphoreType.DMA((2,)),
            pltpu.SemaphoreType.DMA((2,)),
            pltpu.SemaphoreType.DMA((3,)),
            pltpu.SemaphoreType.DMA((3,)),
        ],
        compiler_params=pltpu.CompilerParams(
            vmem_limit_bytes=VMEM_LIMIT, collective_id=1, has_side_effects=True
        ),
    )(
        column_features,
        column_route[None, :],
        cotangent.reshape(region_slots, row_width),
        first_weight,
        second_weight,
    )
    return pl.pallas_call(
        functools.partial(finish_kernel, factor),
        out_shape=(
            jax.ShapeDtypeStruct(cotangent.shape, BF16),
            back_shape,
            grad_shape,
            grad_shape,
        ),
        in_specs=[vmem] * 3,
        out_specs=[vmem] * 4,
        scratch_shapes=[pltpu.VMEM((padded, LANES), F32)],
        compiler_params=params(),
    )(out_rows, back_rows, sums)


def solution(mesh):
    in_specs = (P(("rx", "ry"), None), P(("rx", "ry")), P("rx", "ry", None), P(), P())
    out_specs = (P("rx", "ry", None), P(("rx", "ry"), None), P(), P())
    return jax.shard_map(
        on_device, mesh=mesh, in_specs=in_specs, out_specs=out_specs, check_vma=False
    )
```

```python
import functools

import jax
import jax.numpy as jnp
from jax import lax
from jax.experimental import pallas as pl
from jax.experimental.pallas import tpu as pltpu
from jax.sharding import PartitionSpec as P

F32 = jnp.float32
BF16 = jnp.bfloat16
LANES = 128
VMEM_LIMIT = 64 * 1024 * 1024 - 64 * 1024
SIDES = [(dx, dy) for dx in (-1, 0, 1) for dy in (-1, 0, 1) if (dx, dy) != (0, 0)]


def params():
    return pltpu.CompilerParams(vmem_limit_bytes=VMEM_LIMIT)


def iota(shape, dim):
    return lax.broadcasted_iota(jnp.int32, shape, dim)


def build_move(move, depth):
    width = move.shape[0]
    k = iota((width, 2 * LANES), 0)
    n = iota((width, 2 * LANES), 1)
    base = k - (n % LANES) * depth - n // LANES
    for zp in range(depth // 2):
        move[:, zp * 2 * LANES : (zp + 1) * 2 * LANES] = jnp.where(
            base == 2 * zp, 1.0, 0.0
        ).astype(BF16)


def spread_columns(rows, scale, move, scratch, depth):
    count = rows.shape[0]
    for zp in range(depth // 2):
        moved = jnp.dot(
            rows, move[:, zp * 2 * LANES : (zp + 1) * 2 * LANES], preferred_element_type=F32
        )
        if scale is not None:
            moved = moved * scale
        scratch[pl.ds(2 * zp, count, stride=depth), :] = moved[:, :LANES]
        scratch[pl.ds(2 * zp + 1, count, stride=depth), :] = moved[:, LANES:]


def gather_columns(scratch, move, count, depth):
    wide = jnp.concatenate(
        [scratch[pl.ds(z, count, stride=depth), :] for z in range(depth)], axis=1
    ).astype(BF16)
    return lax.dot_general(
        wide, move[...], (((1,), (1,)), ((), ())), preferred_element_type=F32
    ).astype(BF16)


def shift_block(planes, xs, ys):
    block = planes[1, xs, ys]
    count_x, count_y, depth, lanes = block.shape
    total = count_x * count_y * depth
    z = iota((total, lanes), 0) % depth
    v = block.astype(F32).reshape(total, lanes)
    below = jnp.where(z == 0, 0.0, pltpu.roll(v, 1, 0))
    above = jnp.where(z == depth - 1, 0.0, pltpu.roll(v, total - 1, 0))
    planes[0, xs, ys] = below.astype(BF16).reshape(block.shape)
    planes[2, xs, ys] = above.astype(BF16).reshape(block.shape)


def shift_inside(planes):
    rows, columns = planes.shape[1] - 2, planes.shape[2] - 2

    def body(x, carry):
        shift_block(planes, pl.ds(x + 1, 1), pl.ds(1, columns))
        return carry

    lax.fori_loop(0, rows, body, 0)


def shift_border(planes):
    rows, columns = planes.shape[1] - 2, planes.shape[2] - 2
    shift_block(planes, pl.ds(0, 1), pl.ds(0, columns + 2))
    shift_block(planes, pl.ds(rows + 1, 1), pl.ds(0, columns + 2))
    shift_block(planes, pl.ds(1, rows), pl.ds(0, 1))
    shift_block(planes, pl.ds(1, rows), pl.ds(columns + 1, 1))


def clear_border(planes):
    _, count_x, count_y, depth, lanes = planes.shape
    planes[1, 0] = jnp.zeros((count_y, depth, lanes), BF16)
    planes[1, count_x - 1] = jnp.zeros((count_y, depth, lanes), BF16)
    planes[1, :, 0] = jnp.zeros((count_x, depth, lanes), BF16)
    planes[1, :, count_y - 1] = jnp.zeros((count_x, depth, lanes), BF16)


def pair_weights(weights, table, transposed):
    channels = weights.shape[1]
    table[...] = jnp.zeros(table.shape, BF16)
    for a in range(3):
        for b in range(3):
            for c in range(3):
                tap = 9 * a + 3 * b + c
                if transposed:
                    block = weights[tap].astype(F32).T.astype(BF16)
                else:
                    block = weights[26 - tap]
                for p in range(2):
                    row = ((a + p) * 9 + 3 * b + c) * LANES
                    table[row : row + channels, p * LANES : p * LANES + channels] = block


def pair_conv(planes, table, xp, count_y):
    depth = planes.shape[3]
    pieces = []
    for j in range(4):
        for b in range(3):
            for c in range(3):
                pieces.append(
                    planes[c, 2 * xp + j, b : b + count_y].reshape(count_y * depth, LANES)
                )
    return jnp.dot(jnp.concatenate(pieces, axis=1), table[...], preferred_element_type=F32)


def correlate(local, planes, turned, out):
    _, count_x, count_y, depth, _ = local.shape
    count_x, count_y = count_x - 2, count_y - 2
    rows = count_y * depth
    for xp in range(count_x // 2):
        pair = jnp.concatenate(
            [
                local[1, 2 * xp + 1, 1 : count_y + 1].reshape(rows, LANES),
                local[1, 2 * xp + 2, 1 : count_y + 1].reshape(rows, LANES),
            ],
            axis=1,
        )
        turned[:, xp * rows : (xp + 1) * rows] = pair.astype(F32).T.astype(BF16)
    out[...] = jnp.zeros(out.shape, F32)

    def body(step, carry):
        jj = (step // 3) * 2
        b = step % 3
        pieces = []
        for dj in range(2):
            for c in range(3):
                pieces.append(
                    jnp.concatenate(
                        [
                            planes[c, 2 * xp + jj + dj, pl.ds(b, count_y)].reshape(rows, LANES)
                            for xp in range(count_x // 2)
                        ],
                        axis=0,
                    )
                )
        for half in range(3):
            both = jnp.concatenate([pieces[2 * half], pieces[2 * half + 1]], axis=1)
            prod = jnp.dot(turned[...], both, preferred_element_type=F32)
            for s in range(2):
                dj, c = divmod(2 * half + s, 3)
                for p in range(2):
                    slot = (jj + dj - p + 1) * 9 + 3 * b + c
                    out[slot] += prod[p * LANES : (p + 1) * LANES, s * LANES : (s + 1) * LANES]
        return carry

    lax.fori_loop(0, 6, body, 0)


def pack_grads(out, packed, base, flip, channels):
    tall = channels * channels // LANES
    rest = channels - tall
    lane = iota((tall, LANES), 1)

    def body(k):
        block = out[9 + 26 - k].T if flip else out[9 + k]
        low = block[tall:channels]
        part = LANES - channels
        moved = jnp.concatenate(
            [pltpu.roll(low, channels - part * m, 1) for m in range(tall // rest)], axis=0
        )
        at = pl.ds(pl.multiple_of((base + k) * tall, 8), tall)
        packed[at, :] = jnp.where(lane < channels, block[:tall], moved)

    def three(step, carry):
        for t in range(3):
            body(3 * step + t)
        return carry

    lax.fori_loop(0, 9, three, 0)


def unpack_grads(packed, dest, base, factor, channels):
    tall = channels * channels // LANES
    rest = channels - tall
    part = LANES - channels
    lane = iota((rest, LANES), 1)

    def body(k):
        v = packed[pl.ds(pl.multiple_of((base + k) * tall, 8), tall), :] * factor
        low = jnp.zeros((rest, LANES), F32)
        for m in range(tall // rest):
            turned = pltpu.roll(v[m * rest : (m + 1) * rest], (part * m - channels) % LANES, 1)
            low = jnp.where(lane // part == m, turned, low)
        dest[k, :tall, :] = v[:, :channels]
        dest[k, tall:, :] = low[:, :channels]

    def three(step, carry):
        for t in range(3):
            body(3 * step + t)
        return carry

    lax.fori_loop(0, 9, three, 0)


class Halo:
    def __init__(self, planes, send_sem, recv_sem, grid):
        self.planes, self.send_sem, self.recv_sem, self.grid = planes, send_sem, recv_sem, grid
        self.extent = (planes.shape[1] - 2, planes.shape[2] - 2)

    def copy(self, k):
        source, target = [], []
        for step, extent in zip(SIDES[k], self.extent):
            source.append({0: pl.ds(1, extent), 1: pl.ds(extent, 1), -1: pl.ds(1, 1)}[step])
            target.append({0: pl.ds(1, extent), 1: pl.ds(0, 1), -1: pl.ds(extent + 1, 1)}[step])
        (ix, iy, _, _), (dx, dy) = self.grid, SIDES[k]
        return pltpu.make_async_remote_copy(
            src_ref=self.planes.at[1, source[0], source[1]],
            dst_ref=self.planes.at[1, target[0], target[1]],
            send_sem=self.send_sem.at[k],
            recv_sem=self.recv_sem.at[k],
            device_id=(ix + dx, iy + dy),
            device_id_type=pl.DeviceIdType.MESH,
        )

    def there(self, dx, dy):
        ix, iy, nx, ny = self.grid
        return jnp.logical_and(
            jnp.logical_and(ix + dx >= 0, ix + dx < nx), jnp.logical_and(iy + dy >= 0, iy + dy < ny)
        )

    def start(self):
        for k, (dx, dy) in enumerate(SIDES):

            @pl.when(self.there(dx, dy))
            def _():
                self.copy(k).start()

    def wait(self):
        for k, (dx, dy) in enumerate(SIDES):

            @pl.when(self.there(-dx, -dy))
            def _():
                self.copy(k).wait_recv()

            @pl.when(self.there(dx, dy))
            def _():
                self.copy(k).wait_send()


def lay_messages(parts, scratch, dest):
    devices, height, _ = dest.shape
    pitch = scratch.shape[0] // devices
    for row, value in enumerate(parts):
        scratch[pl.ds(row, devices, stride=pitch), :] = value
    flat = scratch[...].reshape(devices, pitch, LANES)
    dest[...] = flat[:, :height].astype(BF16)


def read_messages(source, scratch, capacity):
    devices, height, _ = source.shape
    pitch = scratch.shape[0] // devices
    each = height // capacity
    filler = jnp.zeros((devices, pitch - height, LANES), F32)
    scratch[...] = jnp.concatenate([source[...].astype(F32), filler], axis=1).reshape(
        scratch.shape
    )
    return jnp.concatenate(
        [
            jnp.concatenate(
                [
                    scratch[pl.ds(k * each + j, devices, stride=pitch), :].astype(BF16)
                    for j in range(each)
                ],
                axis=1,
            )
            for k in range(capacity)
        ],
        axis=0,
    )


def core_kernel(
    nx, ny, capacity,
    feat_ref, route_row_ref, cot_ref, w1_ref, w2_ref,
    out_ref, fg_ref, sum_ref,
    x3, g3, a3, h3, tx, tg, ta, th, move, s1, s2, mask_p, turned, grads,
    packed, shares, spread, whole,
    sent, got, back_sent, back_got, routes,
    halo_send, halo_recv, sum_send, sum_recv, pair_send, pair_recv, col_send, col_recv,
):
    ix, iy = lax.axis_index("rx"), lax.axis_index("ry")
    count = nx * ny
    me = ix * ny + iy
    barrier = pltpu.get_barrier_semaphore()
    mesh_id = pl.DeviceIdType.MESH

    def wrap(value, extent):
        value = jnp.where(value >= extent, value - extent, value)
        return jnp.where(value < 0, value + extent, value)

    def each_peer(visit, stride=1, way=1):
        for dx in range(0, nx, stride):
            px = wrap(ix + way * dx, nx)

            def single(dy):
                visit(dx * ny + dy, px, wrap(iy + way * dy, ny))

            def four(step, carry):
                for k in range(4):
                    single(4 * step + k)
                return carry

            if dx == 0:
                for dy in range(1, 4):
                    single(dy)
            lax.fori_loop(1 if dx == 0 else 0, ny // 4, four, 0)

    for planes in (x3, g3, a3, h3):
        clear_border(planes)

    def greet(d, px, py):
        pl.semaphore_signal(barrier, inc=1, device_id=(px, py), device_id_type=mesh_id)

    each_peer(greet)
    _, count_x, count_y, depth, _ = x3.shape
    count_x, count_y = count_x - 2, count_y - 2
    rows = count_y * depth
    slots, width = cot_ref.shape
    shard = feat_ref.shape[0]
    channels = w1_ref.shape[1]
    grid = (ix, iy, nx, ny)
    halos = [
        Halo(planes, halo_send.at[k], halo_recv.at[k], grid)
        for k, planes in enumerate((x3, g3, a3, h3))
    ]
    inside = (pl.ds(1, count_x), pl.ds(1, count_y))

    row = route_row_ref[...]
    col = jnp.broadcast_to(row.astype(F32), (shard, shard)).T[:, :1].astype(jnp.int32)
    owner_row, owner_col = lax.div(row, slots), lax.div(col, slots)
    same = owner_col == owner_row
    s0, s1_ = iota((shard, shard), 0), iota((shard, shard), 1)
    rank_row = jnp.sum(jnp.where(same & (s0 < s1_), 1.0, 0.0), axis=0, keepdims=True)
    rank_col = jnp.sum(jnp.where(same & (s1_ < s0), 1.0, 0.0), axis=1, keepdims=True)

    def ahead(owner):
        far = lax.rem(lax.div(owner, ny) - ix + nx, nx)
        return far * ny + lax.rem(lax.rem(owner, ny) - iy + ny, ny)

    ahead_row, ahead_col = ahead(owner_row), ahead(owner_col)
    place_row = rank_row.astype(jnp.int32) * count + ahead_row
    place_col = rank_col.astype(jnp.int32) * count + ahead_col
    buffer = capacity * count
    send_hot = jnp.where(iota((buffer, shard), 0) == place_row, 1.0, 0.0).astype(BF16)
    return_hot = jnp.where(iota((shard, buffer), 1) == place_col, 1.0, 0.0).astype(BF16)
    outgoing = jnp.dot(send_hot, feat_ref[...], preferred_element_type=F32)
    lay_messages(
        [
            outgoing[k * count : (k + 1) * count, j * LANES : (j + 1) * LANES]
            for k in range(capacity)
            for j in range(width // LANES)
        ],
        s1,
        sent,
    )
    routes[0] = row
    got[0] = sent[0]
    pl.semaphore_wait(barrier, count - 1)

    def send_route(d, px, py):
        pltpu.make_async_remote_copy(
            src_ref=route_row_ref,
            dst_ref=routes.at[d],
            send_sem=col_send.at[0],
            recv_sem=col_recv.at[0],
            device_id=(px, py),
            device_id_type=mesh_id,
        ).start()

    def send_column(d, px, py):
        pltpu.make_async_remote_copy(
            src_ref=sent.at[d],
            dst_ref=got.at[d],
            send_sem=col_send.at[1],
            recv_sem=col_recv.at[1],
            device_id=(px, py),
            device_id_type=mesh_id,
        ).start()

    def wait_all(ref, sem):
        pltpu.make_async_copy(ref.at[pl.ds(1, count - 1)], ref.at[pl.ds(1, count - 1)], sem).wait()

    each_peer(send_route)
    each_peer(send_column)

    build_move(move, depth)
    spread_columns(cot_ref[...], None, move, s2, depth)
    pair_weights(w2_ref, tg, False)
    wait_all(routes, col_recv.at[0])

    known = routes[...].reshape(count, shard)
    mine = lax.div(known, slots) == me
    mine_f = jnp.where(mine, 1.0, 0.0)
    upper = jnp.where(s0 < s1_, 1.0, 0.0).astype(BF16)
    before = jnp.dot(mine_f.astype(BF16), upper, preferred_element_type=F32)
    slot_of = lax.rem(known, slots).astype(F32)
    slot_cols, slot_rows = [], []
    for k in range(capacity):
        chosen = mine & (before == float(k))
        found = jnp.sum(jnp.where(chosen, slot_of + 1.0, 0.0), axis=1, keepdims=True) - 1.0
        slot_cols.append(found)
        slot_rows.append(jnp.broadcast_to(found, (count, LANES)).T[:1, :])
    slot_row = jnp.concatenate(slot_rows, axis=1).astype(jnp.int32)
    slot_col = jnp.concatenate(slot_cols, axis=0).astype(jnp.int32)
    hot = jnp.where(slot_row == iota((slots, buffer), 0), 1.0, 0.0)
    back_hot = jnp.where(slot_col == iota((buffer, slots), 1), 1.0, 0.0).astype(BF16)
    active = jnp.sum(hot, axis=1, keepdims=True)
    wide = jnp.broadcast_to(active, (slots, LANES))
    for z in range(depth):
        mask_p[pl.ds(z, slots, stride=depth), :] = wide
    g3[1, inside[0], inside[1]] = (
        (s2[...] * mask_p[...]).astype(BF16).reshape(count_x, count_y, depth, LANES)
    )
    halos[1].start()
    shift_inside(g3)
    pair_weights(w1_ref, tx, True)
    halos[1].wait()
    shift_border(g3)

    def conv_to(planes, table, dest):
        def body(xp, carry):
            both = pair_conv(planes, table, xp, count_y)
            for p in range(2):
                at = pl.ds(pl.multiple_of((2 * xp + p) * rows, rows), rows)
                dest[at, :] = both[:, p * LANES : (p + 1) * LANES]
            return carry

        lax.fori_loop(0, count_x // 2, body, 0)

    conv_to(g3, tg, s2)
    wait_all(got, col_recv.at[1])
    arrived = read_messages(got, s1, capacity)
    field_rows = jnp.dot(hot.astype(BF16), arrived, preferred_element_type=F32).astype(BF16)
    spread_columns(field_rows, None, move, s1, depth)
    x3[1, inside[0], inside[1]] = s1[...].astype(BF16).reshape(count_x, count_y, depth, LANES)
    halos[0].start()
    shift_inside(x3)
    pair_weights(w2_ref, ta, True)
    pair_weights(w1_ref, th, False)
    halos[0].wait()
    shift_border(x3)

    z_of = iota((rows, LANES), 0) % depth

    def store_shifted(planes, x, v):
        shape = (count_y, depth, LANES)
        below = jnp.where(z_of == 0, 0.0, pltpu.roll(v, 1, 0))
        above = jnp.where(z_of == depth - 1, 0.0, pltpu.roll(v, rows - 1, 0))
        for c, part in enumerate((below, v, above)):
            planes[c, x, 1 : count_y + 1] = part.astype(BF16).reshape(shape)

    def forward(xp, carry):
        hidden2 = pair_conv(x3, tx, xp, count_y)
        for p in range(2):
            x = 2 * xp + p
            at = pl.ds(pl.multiple_of(x * rows, rows), rows)
            mask = mask_p[at, :]
            hidden = mask * hidden2[:, p * LANES : (p + 1) * LANES]
            s = 1.0 / (1.0 + jnp.exp(-hidden))
            store_shifted(a3, x + 1, hidden * s)
            store_shifted(h3, x + 1, mask * s2[at, :] * s * (1.0 + hidden * (1.0 - s)))
        return carry

    lax.fori_loop(0, count_x // 2, forward, 0)
    halos[3].start()
    halos[2].start()
    used = 27 * channels * channels // LANES
    packed[used:, :] = jnp.zeros((packed.shape[0] - used, LANES), F32)
    core, chip = lax.rem(ix, 2), lax.div(ix, 2) * ny + iy
    chips = count // 2

    def share_of(px, py):
        return lax.rem(px, 2) * chips + lax.div(px, 2) * ny + py

    def send_shares(half, local, planes, flip):
        correlate(local, planes, turned, grads)
        pack_grads(grads, packed, 0, flip, channels)
        shares[half] = packed[...].astype(BF16).reshape(shares.shape[1:])

        def send_share(d, px, py):
            pltpu.make_async_remote_copy(
                src_ref=shares.at[half, share_of(px, py)],
                dst_ref=spread.at[half, d],
                send_sem=sum_send.at[half],
                recv_sem=sum_recv.at[half],
                device_id=(px, py),
                device_id_type=mesh_id,
            ).start()

        each_peer(send_share)

    def send_totals(half):
        wait_all(spread.at[half], sum_recv.at[half])
        mine = core * chips + chip
        total = shares[half, mine].astype(F32)
        total = total + jnp.sum(spread[half, 1:].astype(F32), axis=0)
        whole[half, mine] = total.astype(BF16)

        def send_total(d, px, py):
            pltpu.make_async_remote_copy(
                src_ref=whole.at[half, mine],
                dst_ref=whole.at[half, mine],
                send_sem=sum_send.at[2 + half],
                recv_sem=sum_recv.at[2 + half],
                device_id=(px, py),
                device_id_type=mesh_id,
            ).start()

        each_peer(send_total, stride=2)

    def across(half):
        mine = whole.at[half, pl.ds(core * chips, chips)]
        return pltpu.make_async_remote_copy(
            src_ref=mine,
            dst_ref=mine,
            send_sem=pair_send.at[half],
            recv_sem=pair_recv.at[half],
            device_id=(ix + 1 - 2 * core, iy),
            device_id_type=mesh_id,
        )

    def wait_same_core(half, sem):
        part = whole.at[half, pl.ds(0, chips - 1)]
        pltpu.make_async_copy(part, part, sem).wait()

    send_shares(0, h3, x3, False)
    halos[3].wait()
    shift_border(h3)

    def grad_body(xp, carry):
        both = pair_conv(h3, th, xp, count_y)
        for p in range(2):
            x = 2 * xp + p
            at = pl.ds(pl.multiple_of(x * rows, rows), rows)
            cot = g3[1, x + 1, 1 : count_y + 1].reshape(rows, LANES).astype(F32)
            s2[at, :] = cot + both[:, p * LANES : (p + 1) * LANES]
        return carry

    lax.fori_loop(0, count_x // 2, grad_body, 0)
    grad_rows = gather_columns(s2, move, slots, depth)
    back_rows = jnp.dot(back_hot, grad_rows, preferred_element_type=F32)
    lay_messages(
        [
            back_rows[k * count : (k + 1) * count, j * LANES : (j + 1) * LANES]
            for k in range(capacity)
            for j in range(width // LANES)
        ],
        s1,
        back_sent,
    )
    back_got[0] = back_sent[0]

    def send_back(d, px, py):
        pltpu.make_async_remote_copy(
            src_ref=back_sent.at[d],
            dst_ref=back_got.at[d],
            send_sem=col_send.at[2],
            recv_sem=col_recv.at[2],
            device_id=(px, py),
            device_id_type=mesh_id,
        ).start()

    each_peer(send_back, way=-1)
    send_shares(1, a3, g3, True)
    send_totals(0)
    halos[2].wait()
    shift_border(a3)

    def block_body(xp, carry):
        both = pair_conv(a3, ta, xp, count_y)
        for p in range(2):
            x = 2 * xp + p
            at = pl.ds(pl.multiple_of(x * rows, rows), rows)
            own = x3[1, x + 1, 1 : count_y + 1].reshape(rows, LANES).astype(F32)
            s1[at, :] = own + mask_p[at, :] * both[:, p * LANES : (p + 1) * LANES]
        return carry

    lax.fori_loop(0, count_x // 2, block_body, 0)
    send_totals(1)
    wait_same_core(0, sum_recv.at[2])
    across(0).start()
    out_ref[...] = gather_columns(s1, move, slots, depth)
    wait_all(back_got, col_recv.at[2])
    returned = read_messages(back_got, s2, capacity)
    fg_ref[...] = jnp.dot(return_hot, returned, preferred_element_type=F32).astype(BF16)
    wait_same_core(1, sum_recv.at[3])
    across(1).start()
    wait_all(routes, col_send.at[0])
    wait_all(got, col_send.at[1])
    wait_all(back_got, col_send.at[2])
    across(0).wait()
    sum_ref[0] = whole[0]
    across(1).wait()
    sum_ref[1] = whole[1]
    for half in range(2):
        wait_all(spread.at[half], sum_send.at[half])
        wait_same_core(half, sum_send.at[2 + half])


def finish_kernel(
    factor,
    out_in, fg_in, sum_in,
    out_ref, fg_ref, dw1_ref, dw2_ref,
    v_out, v_fg, v_sum, grads1, grads2, packed, sems,
):
    copies = [
        pltpu.make_async_copy(source, dest, sems.at[k])
        for k, (source, dest) in enumerate(
            (
                (sum_in.at[0], v_sum.at[0]),
                (sum_in.at[1], v_sum.at[1]),
                (out_in, v_out),
                (fg_in, v_fg),
                (v_out, out_ref),
                (v_fg, fg_ref),
                (grads1, dw1_ref),
                (grads2, dw2_ref),
            )
        )
    ]
    for copy in copies[:4]:
        copy.start()
    channels = grads1.shape[1]
    for half, dest in enumerate((grads1, grads2)):
        copies[half].wait()
        packed[...] = v_sum[half].astype(F32).reshape(packed.shape)
        unpack_grads(packed, dest, 0, factor, channels)
        copies[6 + half].start()
        copies[2 + half].wait()
        copies[4 + half].start()
    for copy in copies[4:]:
        copy.wait()


def on_device(column_features, column_route, cotangent, first_weight, second_weight):
    count_x = lax.axis_size("rx")
    count_y = lax.axis_size("ry")
    count_all = count_x * count_y
    shard_rows, row_width = column_features.shape
    region_x, region_y = cotangent.shape[:2]
    channels = first_weight.shape[1]
    depth = row_width // channels
    region_slots = region_x * region_y
    capacity = 2 * shard_rows // count_all
    planes = pltpu.VMEM((3, region_x + 2, region_y + 2, depth, LANES), BF16)
    table = pltpu.VMEM((36 * LANES, 2 * LANES), BF16)
    voxels = region_slots * depth
    flat = pltpu.VMEM((voxels, LANES), F32)
    padded = -(-(27 * channels * channels // LANES) // (16 * count_all)) * 16 * count_all
    share = pltpu.VMEM((2, count_all, padded // count_all, LANES), BF16)
    messages = pltpu.VMEM((count_all, capacity * row_width // LANES, LANES), BF16)
    factor = float(1.0 / (count_all * shard_rows * depth) ** 0.5)
    grad_shape = jax.ShapeDtypeStruct((27, channels, channels), F32)
    vmem = pl.BlockSpec(memory_space=pltpu.VMEM)
    rows_shape = jax.ShapeDtypeStruct((region_slots, row_width), BF16)
    back_shape = jax.ShapeDtypeStruct((shard_rows, row_width), BF16)
    out_rows, back_rows, sums = pl.pallas_call(
        functools.partial(core_kernel, count_x, count_y, capacity),
        out_shape=(
            rows_shape,
            back_shape,
            jax.ShapeDtypeStruct(share.shape, BF16),
        ),
        in_specs=[vmem] * 5,
        out_specs=[vmem] * 3,
        scratch_shapes=[
            planes, planes, planes, planes,
            table, table, table, table,
            pltpu.VMEM((row_width, depth * LANES), BF16),
            flat, flat, flat,
            pltpu.VMEM((2 * LANES, voxels // 2), BF16),
            pltpu.VMEM((45, LANES, LANES), F32),
            pltpu.VMEM((padded, LANES), F32),
            share, share, share,
            messages, messages, messages, messages,
            pltpu.VMEM((count_all, 1, shard_rows), jnp.int32),
            pltpu.SemaphoreType.DMA((4, len(SIDES))),
            pltpu.SemaphoreType.DMA((4, len(SIDES))),
            pltpu.SemaphoreType.DMA((4,)),
            pltpu.SemaphoreType.DMA((4,)),
            pltpu.SemaphoreType.DMA((2,)),
            pltpu.SemaphoreType.DMA((2,)),
            pltpu.SemaphoreType.DMA((3,)),
            pltpu.SemaphoreType.DMA((3,)),
        ],
        compiler_params=pltpu.CompilerParams(
            vmem_limit_bytes=VMEM_LIMIT, collective_id=1, has_side_effects=True
        ),
    )(
        column_features,
        column_route[None, :],
        cotangent.reshape(region_slots, row_width),
        first_weight,
        second_weight,
    )
    anywhere = pl.BlockSpec(memory_space=pl.ANY)
    out_rows, feature_grads, first_grad, second_grad = pl.pallas_call(
        functools.partial(finish_kernel, factor),
        out_shape=(rows_shape, back_shape, grad_shape, grad_shape),
        in_specs=[anywhere] * 3,
        out_specs=[anywhere] * 4,
        scratch_shapes=[
            pltpu.VMEM(rows_shape.shape, BF16),
            pltpu.VMEM(back_shape.shape, BF16),
            pltpu.VMEM(share.shape, BF16),
            pltpu.VMEM(grad_shape.shape, F32),
            pltpu.VMEM(grad_shape.shape, F32),
            pltpu.VMEM((padded, LANES), F32),
            pltpu.SemaphoreType.DMA((8,)),
        ],
        compiler_params=params(),
    )(out_rows, back_rows, sums)
    return out_rows.reshape(cotangent.shape), feature_grads, first_grad, second_grad


def solution(mesh):
    in_specs = (P(("rx", "ry"), None), P(("rx", "ry")), P("rx", "ry", None), P(), P())
    out_specs = (P("rx", "ry", None), P(("rx", "ry"), None), P(), P())
    return jax.shard_map(
        on_device, mesh=mesh, in_specs=in_specs, out_specs=out_specs, check_vma=False
    )
```

```python
import functools

import jax
import jax.numpy as jnp
from jax import lax
from jax.experimental import pallas as pl
from jax.experimental.pallas import tpu as pltpu
from jax.sharding import PartitionSpec as P

F32 = jnp.float32
BF16 = jnp.bfloat16
LANES = 128
VMEM_LIMIT = 64 * 1024 * 1024 - 64 * 1024
SIDES = [(dx, dy) for dx in (-1, 0, 1) for dy in (-1, 0, 1) if (dx, dy) != (0, 0)]


def params():
    return pltpu.CompilerParams(vmem_limit_bytes=VMEM_LIMIT)


def iota(shape, dim):
    return lax.broadcasted_iota(jnp.int32, shape, dim)


def build_move(move, depth):
    width = move.shape[0]
    k = iota((width, 2 * LANES), 0)
    n = iota((width, 2 * LANES), 1)
    base = k - (n % LANES) * depth - n // LANES
    for zp in range(depth // 2):
        move[:, zp * 2 * LANES : (zp + 1) * 2 * LANES] = jnp.where(
            base == 2 * zp, 1.0, 0.0
        ).astype(BF16)


def spread_columns(rows, scale, move, scratch, depth):
    count = rows.shape[0]
    for zp in range(depth // 2):
        moved = jnp.dot(
            rows, move[:, zp * 2 * LANES : (zp + 1) * 2 * LANES], preferred_element_type=F32
        )
        if scale is not None:
            moved = moved * scale
        scratch[pl.ds(2 * zp, count, stride=depth), :] = moved[:, :LANES]
        scratch[pl.ds(2 * zp + 1, count, stride=depth), :] = moved[:, LANES:]


def gather_columns(scratch, move, count, depth):
    wide = jnp.concatenate(
        [scratch[pl.ds(z, count, stride=depth), :] for z in range(depth)], axis=1
    ).astype(BF16)
    return lax.dot_general(
        wide, move[...], (((1,), (1,)), ((), ())), preferred_element_type=F32
    ).astype(BF16)


def shift_block(planes, xs, ys):
    block = planes[1, xs, ys]
    count_x, count_y, depth, lanes = block.shape
    total = count_x * count_y * depth
    z = iota((total, lanes), 0) % depth
    v = block.astype(F32).reshape(total, lanes)
    below = jnp.where(z == 0, 0.0, pltpu.roll(v, 1, 0))
    above = jnp.where(z == depth - 1, 0.0, pltpu.roll(v, total - 1, 0))
    planes[0, xs, ys] = below.astype(BF16).reshape(block.shape)
    planes[2, xs, ys] = above.astype(BF16).reshape(block.shape)


def shift_inside(planes):
    rows, columns = planes.shape[1] - 2, planes.shape[2] - 2

    def body(x, carry):
        shift_block(planes, pl.ds(x + 1, 1), pl.ds(1, columns))
        return carry

    lax.fori_loop(0, rows, body, 0)


def shift_border(planes):
    rows, columns = planes.shape[1] - 2, planes.shape[2] - 2
    shift_block(planes, pl.ds(0, 1), pl.ds(0, columns + 2))
    shift_block(planes, pl.ds(rows + 1, 1), pl.ds(0, columns + 2))
    shift_block(planes, pl.ds(1, rows), pl.ds(0, 1))
    shift_block(planes, pl.ds(1, rows), pl.ds(columns + 1, 1))


def clear_border(planes):
    _, count_x, count_y, depth, lanes = planes.shape
    planes[1, 0] = jnp.zeros((count_y, depth, lanes), BF16)
    planes[1, count_x - 1] = jnp.zeros((count_y, depth, lanes), BF16)
    planes[1, :, 0] = jnp.zeros((count_x, depth, lanes), BF16)
    planes[1, :, count_y - 1] = jnp.zeros((count_x, depth, lanes), BF16)


def pair_weights(weights, table, transposed):
    channels = weights.shape[1]
    table[...] = jnp.zeros(table.shape, BF16)
    for a in range(3):
        for b in range(3):
            for c in range(3):
                tap = 9 * a + 3 * b + c
                if transposed:
                    block = weights[tap].astype(F32).T.astype(BF16)
                else:
                    block = weights[26 - tap]
                for p in range(2):
                    row = ((a + p) * 9 + 3 * b + c) * LANES
                    table[row : row + channels, p * LANES : p * LANES + channels] = block


def pair_conv(planes, table, step, count_y):
    depth = planes.shape[3]
    halves = []
    for h in range(2):
        pieces = []
        for j in range(4):
            for b in range(3):
                for c in range(3):
                    pieces.append(
                        planes[c, 4 * step + 2 * h + j, b : b + count_y].reshape(
                            count_y * depth, LANES
                        )
                    )
        halves.append(jnp.concatenate(pieces, axis=1))
    return jnp.dot(jnp.concatenate(halves, axis=0), table[...], preferred_element_type=F32)


def quarter(both, k):
    rows = both.shape[0] // 2
    h, p = divmod(k, 2)
    return both[h * rows : (h + 1) * rows, p * LANES : (p + 1) * LANES]


def correlate(local, planes, turned, out):
    _, count_x, count_y, depth, _ = local.shape
    count_x, count_y = count_x - 2, count_y - 2
    rows = count_y * depth
    for xp in range(count_x // 2):
        pair = jnp.concatenate(
            [
                local[1, 2 * xp + 1, 1 : count_y + 1].reshape(rows, LANES),
                local[1, 2 * xp + 2, 1 : count_y + 1].reshape(rows, LANES),
            ],
            axis=1,
        )
        turned[:, xp * rows : (xp + 1) * rows] = pair.astype(F32).T.astype(BF16)
    out[...] = jnp.zeros(out.shape, F32)

    def body(step, carry):
        jj = (step // 3) * 2
        b = step % 3
        pieces = []
        for dj in range(2):
            for c in range(3):
                pieces.append(
                    jnp.concatenate(
                        [
                            planes[c, 2 * xp + jj + dj, pl.ds(b, count_y)].reshape(rows, LANES)
                            for xp in range(count_x // 2)
                        ],
                        axis=0,
                    )
                )
        for half in range(3):
            both = jnp.concatenate([pieces[2 * half], pieces[2 * half + 1]], axis=1)
            prod = jnp.dot(turned[...], both, preferred_element_type=F32)
            for s in range(2):
                dj, c = divmod(2 * half + s, 3)
                for p in range(2):
                    slot = (jj + dj - p + 1) * 9 + 3 * b + c
                    out[slot] += prod[p * LANES : (p + 1) * LANES, s * LANES : (s + 1) * LANES]
        return carry

    lax.fori_loop(0, 6, body, 0)


def pack_grads(out, packed, base, flip, channels):
    tall = channels * channels // LANES
    rest = channels - tall
    lane = iota((tall, LANES), 1)

    def body(k):
        block = out[9 + 26 - k].T if flip else out[9 + k]
        low = block[tall:channels]
        part = LANES - channels
        moved = jnp.concatenate(
            [pltpu.roll(low, channels - part * m, 1) for m in range(tall // rest)], axis=0
        )
        at = pl.ds(pl.multiple_of((base + k) * tall, 8), tall)
        packed[at, :] = jnp.where(lane < channels, block[:tall], moved)

    def three(step, carry):
        for t in range(3):
            body(3 * step + t)
        return carry

    lax.fori_loop(0, 9, three, 0)


def unpack_grads(packed, dest, base, factor, channels):
    tall = channels * channels // LANES
    rest = channels - tall
    part = LANES - channels
    lane = iota((rest, LANES), 1)

    def body(k):
        v = packed[pl.ds(pl.multiple_of((base + k) * tall, 8), tall), :] * factor
        low = jnp.zeros((rest, LANES), F32)
        for m in range(tall // rest):
            turned = pltpu.roll(v[m * rest : (m + 1) * rest], (part * m - channels) % LANES, 1)
            low = jnp.where(lane // part == m, turned, low)
        dest[k, :tall, :] = v[:, :channels]
        dest[k, tall:, :] = low[:, :channels]

    def three(step, carry):
        for t in range(3):
            body(3 * step + t)
        return carry

    lax.fori_loop(0, 9, three, 0)


class Halo:
    def __init__(self, planes, send_sem, recv_sem, grid):
        self.planes, self.send_sem, self.recv_sem, self.grid = planes, send_sem, recv_sem, grid
        self.extent = (planes.shape[1] - 2, planes.shape[2] - 2)

    def copy(self, k):
        source, target = [], []
        for step, extent in zip(SIDES[k], self.extent):
            source.append({0: pl.ds(1, extent), 1: pl.ds(extent, 1), -1: pl.ds(1, 1)}[step])
            target.append({0: pl.ds(1, extent), 1: pl.ds(0, 1), -1: pl.ds(extent + 1, 1)}[step])
        (ix, iy, _, _), (dx, dy) = self.grid, SIDES[k]
        return pltpu.make_async_remote_copy(
            src_ref=self.planes.at[1, source[0], source[1]],
            dst_ref=self.planes.at[1, target[0], target[1]],
            send_sem=self.send_sem.at[k],
            recv_sem=self.recv_sem.at[k],
            device_id=(ix + dx, iy + dy),
            device_id_type=pl.DeviceIdType.MESH,
        )

    def there(self, dx, dy):
        ix, iy, nx, ny = self.grid
        return jnp.logical_and(
            jnp.logical_and(ix + dx >= 0, ix + dx < nx), jnp.logical_and(iy + dy >= 0, iy + dy < ny)
        )

    def start(self):
        for k, (dx, dy) in enumerate(SIDES):

            @pl.when(self.there(dx, dy))
            def _():
                self.copy(k).start()

    def wait(self):
        for k, (dx, dy) in enumerate(SIDES):

            @pl.when(self.there(-dx, -dy))
            def _():
                self.copy(k).wait_recv()

            @pl.when(self.there(dx, dy))
            def _():
                self.copy(k).wait_send()


def lay_messages(parts, scratch, dest):
    devices, height, _ = dest.shape
    pitch = scratch.shape[0] // devices
    for row, value in enumerate(parts):
        scratch[pl.ds(row, devices, stride=pitch), :] = value
    flat = scratch[...].reshape(devices, pitch, LANES)
    dest[...] = flat[:, :height].astype(BF16)


def read_messages(source, scratch, capacity):
    devices, height, _ = source.shape
    pitch = scratch.shape[0] // devices
    each = height // capacity
    filler = jnp.zeros((devices, pitch - height, LANES), F32)
    scratch[...] = jnp.concatenate([source[...].astype(F32), filler], axis=1).reshape(
        scratch.shape
    )
    return jnp.concatenate(
        [
            jnp.concatenate(
                [
                    scratch[pl.ds(k * each + j, devices, stride=pitch), :].astype(BF16)
                    for j in range(each)
                ],
                axis=1,
            )
            for k in range(capacity)
        ],
        axis=0,
    )


def core_kernel(
    nx, ny, capacity,
    feat_ref, route_row_ref, cot_ref, w1_ref, w2_ref,
    out_ref, fg_ref, sum_ref,
    x3, g3, a3, h3, tx, tg, ta, th, move, s1, s2, mask_p, turned, grads,
    packed, shares, spread, whole,
    sent, got, back_sent, back_got, routes,
    halo_send, halo_recv, sum_send, sum_recv, pair_send, pair_recv, col_send, col_recv,
):
    ix, iy = lax.axis_index("rx"), lax.axis_index("ry")
    count = nx * ny
    me = ix * ny + iy
    barrier = pltpu.get_barrier_semaphore()
    mesh_id = pl.DeviceIdType.MESH

    def wrap(value, extent):
        value = jnp.where(value >= extent, value - extent, value)
        return jnp.where(value < 0, value + extent, value)

    def each_peer(visit, stride=1, way=1):
        for dx in range(0, nx, stride):
            px = wrap(ix + way * dx, nx)

            def single(dy):
                visit(dx * ny + dy, px, wrap(iy + way * dy, ny))

            def four(step, carry):
                for k in range(4):
                    single(4 * step + k)
                return carry

            if dx == 0:
                for dy in range(1, 4):
                    single(dy)
            lax.fori_loop(1 if dx == 0 else 0, ny // 4, four, 0)

    for planes in (x3, g3, a3, h3):
        clear_border(planes)

    def greet(d, px, py):
        pl.semaphore_signal(barrier, inc=1, device_id=(px, py), device_id_type=mesh_id)

    each_peer(greet)
    _, count_x, count_y, depth, _ = x3.shape
    count_x, count_y = count_x - 2, count_y - 2
    rows = count_y * depth
    slots, width = cot_ref.shape
    shard = feat_ref.shape[0]
    channels = w1_ref.shape[1]
    grid = (ix, iy, nx, ny)
    halos = [
        Halo(planes, halo_send.at[k], halo_recv.at[k], grid)
        for k, planes in enumerate((x3, g3, a3, h3))
    ]
    inside = (pl.ds(1, count_x), pl.ds(1, count_y))

    row = route_row_ref[...]
    col = jnp.broadcast_to(row.astype(F32), (shard, shard)).T[:, :1].astype(jnp.int32)
    owner_row, owner_col = lax.div(row, slots), lax.div(col, slots)
    same = owner_col == owner_row
    s0, s1_ = iota((shard, shard), 0), iota((shard, shard), 1)
    rank_row = jnp.sum(jnp.where(same & (s0 < s1_), 1.0, 0.0), axis=0, keepdims=True)
    rank_col = jnp.sum(jnp.where(same & (s1_ < s0), 1.0, 0.0), axis=1, keepdims=True)

    def ahead(owner):
        far = lax.rem(lax.div(owner, ny) - ix + nx, nx)
        return far * ny + lax.rem(lax.rem(owner, ny) - iy + ny, ny)

    ahead_row, ahead_col = ahead(owner_row), ahead(owner_col)
    place_row = rank_row.astype(jnp.int32) * count + ahead_row
    place_col = rank_col.astype(jnp.int32) * count + ahead_col
    buffer = capacity * count
    send_hot = jnp.where(iota((buffer, shard), 0) == place_row, 1.0, 0.0).astype(BF16)
    return_hot = jnp.where(iota((shard, buffer), 1) == place_col, 1.0, 0.0).astype(BF16)
    outgoing = jnp.dot(send_hot, feat_ref[...], preferred_element_type=F32)
    lay_messages(
        [
            outgoing[k * count : (k + 1) * count, j * LANES : (j + 1) * LANES]
            for k in range(capacity)
            for j in range(width // LANES)
        ],
        s1,
        sent,
    )
    routes[0] = row
    got[0] = sent[0]
    pl.semaphore_wait(barrier, count - 1)

    def send_route(d, px, py):
        pltpu.make_async_remote_copy(
            src_ref=route_row_ref,
            dst_ref=routes.at[d],
            send_sem=col_send.at[0],
            recv_sem=col_recv.at[0],
            device_id=(px, py),
            device_id_type=mesh_id,
        ).start()

    def send_column(d, px, py):
        pltpu.make_async_remote_copy(
            src_ref=sent.at[d],
            dst_ref=got.at[d],
            send_sem=col_send.at[1],
            recv_sem=col_recv.at[1],
            device_id=(px, py),
            device_id_type=mesh_id,
        ).start()

    def wait_all(ref, sem):
        pltpu.make_async_copy(ref.at[pl.ds(1, count - 1)], ref.at[pl.ds(1, count - 1)], sem).wait()

    each_peer(send_route)
    each_peer(send_column)

    build_move(move, depth)
    spread_columns(cot_ref[...], None, move, s2, depth)
    pair_weights(w2_ref, tg, False)
    wait_all(routes, col_recv.at[0])

    known = routes[...].reshape(count, shard)
    mine = lax.div(known, slots) == me
    mine_f = jnp.where(mine, 1.0, 0.0)
    upper = jnp.where(s0 < s1_, 1.0, 0.0).astype(BF16)
    before = jnp.dot(mine_f.astype(BF16), upper, preferred_element_type=F32)
    slot_of = lax.rem(known, slots).astype(F32)
    slot_cols, slot_rows = [], []
    for k in range(capacity):
        chosen = mine & (before == float(k))
        found = jnp.sum(jnp.where(chosen, slot_of + 1.0, 0.0), axis=1, keepdims=True) - 1.0
        slot_cols.append(found)
        slot_rows.append(jnp.broadcast_to(found, (count, LANES)).T[:1, :])
    slot_row = jnp.concatenate(slot_rows, axis=1).astype(jnp.int32)
    slot_col = jnp.concatenate(slot_cols, axis=0).astype(jnp.int32)
    hot = jnp.where(slot_row == iota((slots, buffer), 0), 1.0, 0.0)
    back_hot = jnp.where(slot_col == iota((buffer, slots), 1), 1.0, 0.0).astype(BF16)
    active = jnp.sum(hot, axis=1, keepdims=True)
    wide = jnp.broadcast_to(active, (slots, LANES))
    for z in range(depth):
        mask_p[pl.ds(z, slots, stride=depth), :] = wide
    g3[1, inside[0], inside[1]] = (
        (s2[...] * mask_p[...]).astype(BF16).reshape(count_x, count_y, depth, LANES)
    )
    halos[1].start()
    shift_inside(g3)
    pair_weights(w1_ref, tx, True)
    halos[1].wait()
    shift_border(g3)

    def conv_to(planes, table, dest):
        def body(xp, carry):
            both = pair_conv(planes, table, xp, count_y)
            for p in range(4):
                at = pl.ds(pl.multiple_of((4 * xp + p) * rows, rows), rows)
                dest[at, :] = quarter(both, p)
            return carry

        lax.fori_loop(0, count_x // 4, body, 0)

    conv_to(g3, tg, s2)
    wait_all(got, col_recv.at[1])
    arrived = read_messages(got, s1, capacity)
    field_rows = jnp.dot(hot.astype(BF16), arrived, preferred_element_type=F32).astype(BF16)
    spread_columns(field_rows, None, move, s1, depth)
    x3[1, inside[0], inside[1]] = s1[...].astype(BF16).reshape(count_x, count_y, depth, LANES)
    halos[0].start()
    shift_inside(x3)
    pair_weights(w2_ref, ta, True)
    pair_weights(w1_ref, th, False)
    halos[0].wait()
    shift_border(x3)

    z_of = iota((rows, LANES), 0) % depth

    def store_shifted(planes, x, v):
        shape = (count_y, depth, LANES)
        below = jnp.where(z_of == 0, 0.0, pltpu.roll(v, 1, 0))
        above = jnp.where(z_of == depth - 1, 0.0, pltpu.roll(v, rows - 1, 0))
        for c, part in enumerate((below, v, above)):
            planes[c, x, 1 : count_y + 1] = part.astype(BF16).reshape(shape)

    def forward(xp, carry):
        hidden2 = pair_conv(x3, tx, xp, count_y)
        for p in range(4):
            x = 4 * xp + p
            at = pl.ds(pl.multiple_of(x * rows, rows), rows)
            mask = mask_p[at, :]
            hidden = mask * quarter(hidden2, p)
            s = 1.0 / (1.0 + jnp.exp(-hidden))
            store_shifted(a3, x + 1, hidden * s)
            store_shifted(h3, x + 1, mask * s2[at, :] * s * (1.0 + hidden * (1.0 - s)))
        return carry

    lax.fori_loop(0, count_x // 4, forward, 0)
    halos[3].start()
    halos[2].start()
    used = 27 * channels * channels // LANES
    packed[used:, :] = jnp.zeros((packed.shape[0] - used, LANES), F32)
    core, chip = lax.rem(ix, 2), lax.div(ix, 2) * ny + iy
    chips = count // 2

    def share_of(px, py):
        return lax.rem(px, 2) * chips + lax.div(px, 2) * ny + py

    def send_shares(half, local, planes, flip):
        correlate(local, planes, turned, grads)
        pack_grads(grads, packed, 0, flip, channels)
        shares[half] = packed[...].astype(BF16).reshape(shares.shape[1:])

        def send_share(d, px, py):
            pltpu.make_async_remote_copy(
                src_ref=shares.at[half, share_of(px, py)],
                dst_ref=spread.at[half, d],
                send_sem=sum_send.at[half],
                recv_sem=sum_recv.at[half],
                device_id=(px, py),
                device_id_type=mesh_id,
            ).start()

        each_peer(send_share)

    def send_totals(half):
        wait_all(spread.at[half], sum_recv.at[half])
        mine = core * chips + chip
        total = shares[half, mine].astype(F32)
        total = total + jnp.sum(spread[half, 1:].astype(F32), axis=0)
        whole[half, mine] = total.astype(BF16)

        def send_total(d, px, py):
            pltpu.make_async_remote_copy(
                src_ref=whole.at[half, mine],
                dst_ref=whole.at[half, mine],
                send_sem=sum_send.at[2 + half],
                recv_sem=sum_recv.at[2 + half],
                device_id=(px, py),
                device_id_type=mesh_id,
            ).start()

        each_peer(send_total, stride=2)

    def across(half):
        mine = whole.at[half, pl.ds(core * chips, chips)]
        return pltpu.make_async_remote_copy(
            src_ref=mine,
            dst_ref=mine,
            send_sem=pair_send.at[half],
            recv_sem=pair_recv.at[half],
            device_id=(ix + 1 - 2 * core, iy),
            device_id_type=mesh_id,
        )

    def wait_same_core(half, sem):
        part = whole.at[half, pl.ds(0, chips - 1)]
        pltpu.make_async_copy(part, part, sem).wait()

    send_shares(0, h3, x3, False)
    halos[3].wait()
    shift_border(h3)

    def grad_body(xp, carry):
        both = pair_conv(h3, th, xp, count_y)
        for p in range(4):
            x = 4 * xp + p
            at = pl.ds(pl.multiple_of(x * rows, rows), rows)
            cot = g3[1, x + 1, 1 : count_y + 1].reshape(rows, LANES).astype(F32)
            s2[at, :] = cot + quarter(both, p)
        return carry

    lax.fori_loop(0, count_x // 4, grad_body, 0)
    grad_rows = gather_columns(s2, move, slots, depth)
    back_rows = jnp.dot(back_hot, grad_rows, preferred_element_type=F32)
    lay_messages(
        [
            back_rows[k * count : (k + 1) * count, j * LANES : (j + 1) * LANES]
            for k in range(capacity)
            for j in range(width // LANES)
        ],
        s1,
        back_sent,
    )
    back_got[0] = back_sent[0]

    def send_back(d, px, py):
        pltpu.make_async_remote_copy(
            src_ref=back_sent.at[d],
            dst_ref=back_got.at[d],
            send_sem=col_send.at[2],
            recv_sem=col_recv.at[2],
            device_id=(px, py),
            device_id_type=mesh_id,
        ).start()

    each_peer(send_back, way=-1)
    send_shares(1, a3, g3, True)
    send_totals(0)
    halos[2].wait()
    shift_border(a3)

    def block_body(xp, carry):
        both = pair_conv(a3, ta, xp, count_y)
        for p in range(4):
            x = 4 * xp + p
            at = pl.ds(pl.multiple_of(x * rows, rows), rows)
            own = x3[1, x + 1, 1 : count_y + 1].reshape(rows, LANES).astype(F32)
            s1[at, :] = own + mask_p[at, :] * quarter(both, p)
        return carry

    lax.fori_loop(0, count_x // 4, block_body, 0)
    send_totals(1)
    wait_same_core(0, sum_recv.at[2])
    across(0).start()
    out_ref[...] = gather_columns(s1, move, slots, depth)
    wait_all(back_got, col_recv.at[2])
    returned = read_messages(back_got, s2, capacity)
    fg_ref[...] = jnp.dot(return_hot, returned, preferred_element_type=F32).astype(BF16)
    wait_same_core(1, sum_recv.at[3])
    across(1).start()
    wait_all(routes, col_send.at[0])
    wait_all(got, col_send.at[1])
    wait_all(back_got, col_send.at[2])
    across(0).wait()
    sum_ref[0] = whole[0]
    across(1).wait()
    sum_ref[1] = whole[1]
    for half in range(2):
        wait_all(spread.at[half], sum_send.at[half])
        wait_same_core(half, sum_send.at[2 + half])


def finish_kernel(
    factor,
    out_in, fg_in, sum_in,
    out_ref, fg_ref, dw1_ref, dw2_ref,
    v_out, v_fg, v_sum, grads1, grads2, packed, sems,
):
    copies = [
        pltpu.make_async_copy(source, dest, sems.at[k])
        for k, (source, dest) in enumerate(
            (
                (sum_in.at[0], v_sum.at[0]),
                (sum_in.at[1], v_sum.at[1]),
                (out_in, v_out),
                (fg_in, v_fg),
                (v_out, out_ref),
                (v_fg, fg_ref),
                (grads1, dw1_ref),
                (grads2, dw2_ref),
            )
        )
    ]
    for copy in copies[:4]:
        copy.start()
    channels = grads1.shape[1]
    for half, dest in enumerate((grads1, grads2)):
        copies[half].wait()
        packed[...] = v_sum[half].astype(F32).reshape(packed.shape)
        unpack_grads(packed, dest, 0, factor, channels)
        copies[6 + half].start()
        copies[2 + half].wait()
        copies[4 + half].start()
    for copy in copies[4:]:
        copy.wait()


def on_device(column_features, column_route, cotangent, first_weight, second_weight):
    count_x = lax.axis_size("rx")
    count_y = lax.axis_size("ry")
    count_all = count_x * count_y
    shard_rows, row_width = column_features.shape
    region_x, region_y = cotangent.shape[:2]
    channels = first_weight.shape[1]
    depth = row_width // channels
    region_slots = region_x * region_y
    capacity = 2 * shard_rows // count_all
    planes = pltpu.VMEM((3, region_x + 2, region_y + 2, depth, LANES), BF16)
    table = pltpu.VMEM((36 * LANES, 2 * LANES), BF16)
    voxels = region_slots * depth
    flat = pltpu.VMEM((voxels, LANES), F32)
    padded = -(-(27 * channels * channels // LANES) // (16 * count_all)) * 16 * count_all
    share = pltpu.VMEM((2, count_all, padded // count_all, LANES), BF16)
    messages = pltpu.VMEM((count_all, capacity * row_width // LANES, LANES), BF16)
    factor = float(1.0 / (count_all * shard_rows * depth) ** 0.5)
    grad_shape = jax.ShapeDtypeStruct((27, channels, channels), F32)
    vmem = pl.BlockSpec(memory_space=pltpu.VMEM)
    rows_shape = jax.ShapeDtypeStruct((region_slots, row_width), BF16)
    back_shape = jax.ShapeDtypeStruct((shard_rows, row_width), BF16)
    out_rows, back_rows, sums = pl.pallas_call(
        functools.partial(core_kernel, count_x, count_y, capacity),
        out_shape=(
            rows_shape,
            back_shape,
            jax.ShapeDtypeStruct(share.shape, BF16),
        ),
        in_specs=[vmem] * 5,
        out_specs=[vmem] * 3,
        scratch_shapes=[
            planes, planes, planes, planes,
            table, table, table, table,
            pltpu.VMEM((row_width, depth * LANES), BF16),
            flat, flat, flat,
            pltpu.VMEM((2 * LANES, voxels // 2), BF16),
            pltpu.VMEM((45, LANES, LANES), F32),
            pltpu.VMEM((padded, LANES), F32),
            share, share, share,
            messages, messages, messages, messages,
            pltpu.VMEM((count_all, 1, shard_rows), jnp.int32),
            pltpu.SemaphoreType.DMA((4, len(SIDES))),
            pltpu.SemaphoreType.DMA((4, len(SIDES))),
            pltpu.SemaphoreType.DMA((4,)),
            pltpu.SemaphoreType.DMA((4,)),
            pltpu.SemaphoreType.DMA((2,)),
            pltpu.SemaphoreType.DMA((2,)),
            pltpu.SemaphoreType.DMA((3,)),
            pltpu.SemaphoreType.DMA((3,)),
        ],
        compiler_params=pltpu.CompilerParams(
            vmem_limit_bytes=VMEM_LIMIT, collective_id=1, has_side_effects=True
        ),
    )(
        column_features,
        column_route[None, :],
        cotangent.reshape(region_slots, row_width),
        first_weight,
        second_weight,
    )
    anywhere = pl.BlockSpec(memory_space=pl.ANY)
    out_rows, feature_grads, first_grad, second_grad = pl.pallas_call(
        functools.partial(finish_kernel, factor),
        out_shape=(rows_shape, back_shape, grad_shape, grad_shape),
        in_specs=[anywhere] * 3,
        out_specs=[anywhere] * 4,
        scratch_shapes=[
            pltpu.VMEM(rows_shape.shape, BF16),
            pltpu.VMEM(back_shape.shape, BF16),
            pltpu.VMEM(share.shape, BF16),
            pltpu.VMEM(grad_shape.shape, F32),
            pltpu.VMEM(grad_shape.shape, F32),
            pltpu.VMEM((padded, LANES), F32),
            pltpu.SemaphoreType.DMA((8,)),
        ],
        compiler_params=params(),
    )(out_rows, back_rows, sums)
    return out_rows.reshape(cotangent.shape), feature_grads, first_grad, second_grad


def solution(mesh):
    in_specs = (P(("rx", "ry"), None), P(("rx", "ry")), P("rx", "ry", None), P(), P())
    out_specs = (P("rx", "ry", None), P(("rx", "ry"), None), P(), P())
    return jax.shard_map(
        on_device, mesh=mesh, in_specs=in_specs, out_specs=out_specs, check_vma=False
    )
```
